128 devices in a mesh: row: 16 (over z, x), vec: 8 (over y, core).
Axes of the slice: x: 4, y: 4, z: 4, core: 2. Of those that a mesh axis runs over, the one named last changes fastest.
Arguments:
- vectors: float32 [32768, 1024], P('row', 'vec'), may hold values from -8 to 8
- hamiltonian: float32 [256, 12, 128, 128], P('row'), may hold values from -0.15 to 0.15, as said below
- column_blocks: int32 [256, 12], P('row'), may hold values from 0 to 255, as said below
- live_counts: int32 [256], P('row'), may hold values from 3 to 12
- lower_bound: float32 [1], replicated, may hold values from -0.85 to -0.65
- upper_bound: float32 [1], replicated, may hold values from 1.05 to 1.3
Outputs:
- filtered: float32 [32768, 1024], P('row', 'vec')
The draws below stay inside these ranges and needn't reach their ends.
Inputs may be any that keep to these rules, and one draw needn't show every extreme that they name: column_blocks[i, 0] = i, and every entry lies within 16 block rows of its row i, cyclically modulo 256; the distances 16 and -16 both occur. `hamiltonian`: H is symmetric: for every used slot of block row i that names column block j there is a used slot of block row j that names i and holds the transpose of its block, and slot 0 of every block row holds a symmetric block.
All inputs are finite; a program needn't handle non-finite values.
Results may differ from the reference program's by a relative error of at most 0.0003.
Values sent between devices are 32-bit elements; how exact they have to be, the bound alone decides.
No kernel may reach another device: no remote copies, remote signals or barrier semaphores. Data moves between devices by JAX's collectives and lax.ppermute only.
A program may use at most 128 MiB of HBM per device.

```python
import math
import jax
import jax.numpy as jnp
from jax import lax

B = 128
K = 12
NV = 1024
NS_ITERS = 3
BR_DEV = 16
NB = 256
ROWS = 32768


def build_pattern(key):
    pattern_key = jax.random.fold_in(key, 7001)
    key_dist, key_centre, key_live, key_match = jax.random.split(pattern_key, 4)
    layer_count = (K - 2) // 2
    distances = jax.random.randint(key_dist, (layer_count,), 1, BR_DEV + 1).astype(jnp.int32)
    centre = jax.random.randint(key_centre, (), 0, NB).astype(jnp.int32)
    row_ids = jnp.arange(NB, dtype=jnp.int32)
    half_rows = NB // 2
    distance_to = jnp.abs(row_ids - centre)
    distance_to = jnp.minimum(distance_to, NB - distance_to)
    nearness = (half_rows - distance_to) * 1000 // half_rows
    weight_level = nearness * nearness // 1000
    weight_level = weight_level * weight_level // 1000
    threshold = 50 + 950 * weight_level // 1000
    live_draws = jax.random.randint(key_live, (layer_count, NB), 0, 1000)
    shift_live = (live_draws < threshold[None, :]).astype(jnp.int32)
    shift_live = shift_live.at[0].set(1)
    partner = jnp.where(row_ids // BR_DEV % 2 == 0, row_ids + BR_DEV, row_ids - BR_DEV).astype(jnp.int32)
    lower_end = jnp.minimum(row_ids, partner)
    match_draws = jax.random.randint(key_match, (NB,), 0, 1000)
    match_live = (match_draws < threshold).astype(jnp.int32)
    layer_ids = jnp.arange(layer_count, dtype=jnp.int32)
    antipode = (centre + half_rows) % NB
    anti_minus = (antipode - distances) % NB
    shift_live = shift_live.at[layer_ids[1:], antipode].set(0)
    shift_live = shift_live.at[layer_ids[1:], anti_minus[1:]].set(0)
    match_live = match_live.at[lower_end[antipode]].set(0)
    centre_minus = (centre - distances) % NB
    shift_live = shift_live.at[layer_ids, centre].set(1)
    shift_live = shift_live.at[layer_ids, centre_minus].set(1)
    match_live = match_live.at[lower_end[centre]].set(1)
    plus_targets = (row_ids[:, None] + distances[None, :]) % NB
    minus_targets = (row_ids[:, None] - distances[None, :]) % NB
    targets = jnp.concatenate([row_ids[:, None], plus_targets, minus_targets, partner[:, None]], axis=1)
    plus_flags = shift_live.T
    minus_flags = shift_live[layer_ids[None, :], minus_targets]
    match_flags = match_live[lower_end][:, None]
    live_flags = jnp.concatenate([jnp.ones((NB, 1), jnp.int32), plus_flags, minus_flags, match_flags], axis=1)
    order_key = (1 - live_flags) * 16 + jnp.arange(K, dtype=jnp.int32)[None, :]
    slot_order = jnp.argsort(order_key, axis=1, stable=True).astype(jnp.int32)
    column_blocks = jnp.take_along_axis(targets, slot_order, axis=1).astype(jnp.int32)
    live_counts = jnp.sum(live_flags, axis=1).astype(jnp.int32)
    return (distances, partner, lower_end, minus_targets, slot_order, column_blocks, live_counts)


def draw_column_blocks(key, part):
    pattern = build_pattern(key)
    return pattern[5]


def draw_live_counts(key, part):
    pattern = build_pattern(key)
    return pattern[6]


def draw_hamiltonian(key, part):
    distances, partner, lower_end, minus_targets, slot_order, unused_cols, unused_counts = build_pattern(key)
    block_key = jax.random.fold_in(key, 7002)
    key_shift, key_match, key_self = jax.random.split(block_key, 3)
    layer_count = (K - 2) // 2
    block_scale = (4.0 * B * K) ** (-0.5)

    def entries(sub_key, array_shape):
        return jax.random.normal(sub_key, array_shape, jnp.float32)
    shift_blocks = entries(key_shift, (layer_count, NB, B, B))
    match_blocks = entries(key_match, (NB, B, B))
    self_raw = entries(key_self, (NB, B, B))
    row_ids = jnp.arange(NB, dtype=jnp.int32)
    layer_ids = jnp.arange(layer_count, dtype=jnp.int32)
    plus_blocks = jnp.moveaxis(shift_blocks, 0, 1)
    minus_blocks = jnp.swapaxes(shift_blocks[layer_ids[None, :], minus_targets], -1, -2)
    match_picked = match_blocks[lower_end]
    is_lower = (row_ids == lower_end)[:, None, None]
    match_side = jnp.where(is_lower, match_picked, jnp.swapaxes(match_picked, -1, -2))
    self_blocks = (self_raw + jnp.swapaxes(self_raw, -1, -2)) / math.sqrt(2.0)
    assembled = jnp.concatenate([self_blocks[:, None], plus_blocks, minus_blocks, match_side[:, None]], axis=1)
    assembled = jnp.clip(assembled * block_scale, -0.15, 0.15)
    return jnp.take_along_axis(assembled, slot_order[:, :, None, None], axis=1).astype(jnp.float32)


def draw_vectors(key, part):
    vector_key = jax.random.fold_in(key, 7003)
    key_base, key_mix = jax.random.split(vector_key, 2)
    base_rows = jax.random.normal(key_base, (ROWS, NV), jnp.float32)
    mixing = jax.random.normal(key_mix, (NV, NV), jnp.float32) * (0.5 / math.sqrt(NV))
    mixing = mixing + jnp.eye(NV, dtype=jnp.float32)
    mixed = jnp.dot(base_rows, mixing, precision=lax.Precision.HIGHEST)
    return jnp.clip(mixed, -8.0, 8.0).astype(jnp.float32)


def setup_inputs(seed: int = 0) -> dict:
    streams_of = jax.random.split(jax.random.key(seed), 7)
    vectors = draw_vectors(jax.random.fold_in(streams_of[6], 71), 0)
    hamiltonian = draw_hamiltonian(jax.random.fold_in(streams_of[6], 71), 0)
    column_blocks = draw_column_blocks(jax.random.fold_in(streams_of[6], 71), 0)
    live_counts = draw_live_counts(jax.random.fold_in(streams_of[6], 71), 0)
    lower_bound = jnp.clip(jax.random.uniform(streams_of[4], (1,), jnp.float32, -0.85, -0.65), -0.85, -0.65)
    upper_bound = jnp.clip(jax.random.uniform(streams_of[5], (1,), jnp.float32, 1.05, 1.3), 1.05, 1.3)
    return dict(vectors=vectors, hamiltonian=hamiltonian, column_blocks=column_blocks, live_counts=live_counts, lower_bound=lower_bound, upper_bound=upper_bound)


def apply_field(operand, hamiltonian, column_blocks, live_counts):
    blocks = operand.reshape(NB, B, NV)

    def add_slot(summed, inputs):
        matrix, targets, slot_index = inputs
        picked = jnp.take(blocks, targets, axis=0)
        live_mask = (slot_index < live_counts).astype(jnp.float32)
        summed = summed + jnp.einsum('rij,rjc->ric', matrix, picked * live_mask[:, None, None], precision=lax.Precision.HIGHEST)
        return (summed, None)
    inputs = (jnp.moveaxis(hamiltonian, 1, 0), column_blocks.T, jnp.arange(K, dtype=jnp.int32))
    summed, unused = lax.scan(add_slot, jnp.zeros((NB, B, NV), jnp.float32), inputs)
    return summed.reshape(ROWS, NV)

def reference(vectors, hamiltonian, column_blocks, live_counts, lower_bound, upper_bound):
    centre = (upper_bound[0] + lower_bound[0]) / 2
    radius = (upper_bound[0] - lower_bound[0]) / 2
    first = (apply_field(vectors, hamiltonian, column_blocks, live_counts) - centre * vectors) / radius
    second = 2 * (apply_field(first, hamiltonian, column_blocks, live_counts) - centre * first) / radius - vectors
    energy = jnp.sum(second * second)
    current = second * jnp.sqrt(NV / (4 * (energy + 1e-06)))
    for iteration in range(NS_ITERS):
        gram = jnp.einsum('rc,rd->cd', current, current, precision=lax.Precision.HIGHEST)
        current = 1.5 * current - 0.5 * jnp.dot(current, gram, precision=lax.Precision.HIGHEST, preferred_element_type=jnp.float32)
    return current * math.sqrt(ROWS)
```

```python
import math

import jax
import jax.numpy as jnp
from jax import lax
from jax.sharding import PartitionSpec as P

NV = 1024
NS_ITERS = 3
PREC = lax.Precision.HIGH


def halo(cells, width):
    count = lax.axis_size("row")
    head = cells[:width]
    tail = cells[cells.shape[0] - width :]
    return jnp.concatenate(
        [
            lax.ppermute(tail, "row", [(i, (i + 1) % count) for i in range(count)]),
            cells,
            lax.ppermute(head, "row", [((i + 1) % count, i) for i in range(count)]),
        ],
        axis=0,
    )


def dot(a, b):
    return jnp.dot(a, b, precision=PREC, preferred_element_type=jnp.float32)


def on_device(vectors, hamiltonian, column_blocks, live_counts, lower_bound, upper_bound):
    rows_dev, panel_cols = vectors.shape
    block_rows, slot_count, block_size, unused_size = hamiltonian.shape
    row_count = lax.axis_size("row")
    first_row = lax.axis_index("row") * block_rows
    local_cols = (column_blocks - first_row + block_rows) % (block_rows * row_count)
    live_mask = (
        jnp.arange(slot_count, dtype=jnp.int32)[None, :] < live_counts[:, None]
    ).astype(jnp.float32)

    def apply_field(operand):
        widened = halo(operand, block_rows * block_size)
        widened_blocks = widened.reshape(3 * block_rows, block_size, panel_cols)
        picked = jnp.take(widened_blocks, local_cols, axis=0)
        summed = jnp.einsum(
            "rkij,rkjc->ric",
            hamiltonian,
            picked * live_mask[:, :, None, None],
            precision=PREC,
            preferred_element_type=jnp.float32,
        )
        return summed.reshape(rows_dev, panel_cols)

    centre = (upper_bound[0] + lower_bound[0]) / 2
    radius = (upper_bound[0] - lower_bound[0]) / 2
    first = (apply_field(vectors) - centre * vectors) / radius
    second = 2 * (apply_field(first) - centre * first) / radius - vectors
    stacked = lax.all_to_all(second, "vec", split_axis=0, concat_axis=1, tiled=True)
    local_gram = jnp.einsum(
        "rc,rd->cd", stacked, stacked, precision=PREC, preferred_element_type=jnp.float32
    )
    gram = lax.psum(local_gram, ("row", "vec"))
    energy = jnp.trace(gram)
    scale = jnp.sqrt(NV / (4 * (energy + 1e-06)))
    gram = gram * (scale * scale)
    eye = jnp.eye(NV, dtype=jnp.float32)
    out = stacked
    for iteration in range(NS_ITERS):
        step = 1.5 * eye - 0.5 * gram
        out = dot(out, step)
        if iteration + 1 < NS_ITERS:
            gram = dot(step, dot(gram, step))
    out = out * (scale * math.sqrt(rows_dev * row_count))
    return lax.all_to_all(out, "vec", split_axis=1, concat_axis=0, tiled=True)


def solution(mesh):
    placed = (P("row", "vec"), P("row", None, None, None), P("row", None), P("row"), P(), P())
    return jax.shard_map(
        on_device, mesh=mesh, in_specs=placed, out_specs=P("row", "vec"), check_vma=False
    )
```

```python
import functools
import math

import jax
import jax.numpy as jnp
from jax import lax
from jax.experimental import pallas as pl
from jax.experimental.pallas import tpu as pltpu
from jax.sharding import PartitionSpec as P

NV = 1024
BF = jnp.bfloat16
F32 = jnp.float32
VMEM_LIMIT = 56 * 1024 * 1024


def split(x):
    high = x.astype(BF)
    return high, (x - high.astype(F32)).astype(BF)


def fold(full):
    rows, cols = full.shape[0] // 2, full.shape[1] // 2
    return (full[:rows, :cols] + full[rows:, :cols]) + (full[:rows, cols:] + full[rows:, cols:])


def mm(a, b):
    return jnp.dot(a, b, preferred_element_type=F32)


def cost(flops, moved):
    return pl.CostEstimate(flops=flops, bytes_accessed=moved, transcendentals=0)


def split_kernel(h_ref, o_ref):
    high, low = split(h_ref[0])
    o_ref[0, :, :128, :] = high
    o_ref[0, :, 128:, :] = low


def split_blocks(hamiltonian):
    block_rows, slots, size, _ = hamiltonian.shape
    return pl.pallas_call(
        split_kernel,
        out_shape=jax.ShapeDtypeStruct((block_rows, slots, 2 * size, size), BF),
        grid=(block_rows,),
        in_specs=[pl.BlockSpec((1, slots, size, size), lambda i: (i, 0, 0, 0))],
        out_specs=pl.BlockSpec((1, slots, 2 * size, size), lambda i: (i, 0, 0, 0)),
        compiler_params=pltpu.CompilerParams(vmem_limit_bytes=VMEM_LIMIT),
        cost_estimate=cost(0, 8 * block_rows * slots * size * size),
        name="split_blocks",
    )(hamiltonian)


def field_kernel(slots, second, cols_ref, coef_ref, h_ref, left_ref, own_ref, right_ref, *rest):
    if second:
        prev_ref, o_ref, wide = rest
    else:
        o_ref, wide = rest
    i = pl.program_id(0)
    count = own_ref.shape[0]

    @pl.when(i == 0)
    def _():
        for part, ref in enumerate((left_ref, own_ref, right_ref)):

            @pl.loop(0, count)
            def _(j):
                high, low = split(ref[j])
                wide[part * count + j, :, :128] = high
                wide[part * count + j, :, 128:] = low

        wide[3 * count] = jnp.zeros(wide.shape[1:], BF)

    lhs = jnp.concatenate([h_ref[0, k] for k in range(slots)], axis=1)
    rhs = jnp.concatenate([wide[cols_ref[i * slots + k]] for k in range(slots)], axis=0)
    summed = fold(mm(lhs, rhs))
    centre, inverse = coef_ref[0], coef_ref[1]
    result = (summed - centre * own_ref[i]) * inverse
    if second:
        result = 2.0 * result - prev_ref[i]
    o_ref[0] = result


def apply_field(second, cols, coef, split_h, left, own, right, prev=None):
    block_rows, slots, double, size = split_h.shape
    whole = pl.BlockSpec((block_rows, size, size), lambda i, *_: (0, 0, 0))
    operands = [split_h, left, own, right] + ([prev] if second else [])
    return pl.pallas_call(
        functools.partial(field_kernel, slots, second),
        out_shape=jax.ShapeDtypeStruct((block_rows, size, size), F32),
        grid_spec=pltpu.PrefetchScalarGridSpec(
            num_scalar_prefetch=2,
            grid=(block_rows,),
            in_specs=[pl.BlockSpec((1, slots, double, size), lambda i, *_: (i, 0, 0, 0))]
            + [whole] * (len(operands) - 1),
            out_specs=pl.BlockSpec((1, size, size), lambda i, *_: (i, 0, 0)),
            scratch_shapes=[pltpu.VMEM((3 * block_rows + 1, size, 2 * size), BF)],
        ),
        compiler_params=pltpu.CompilerParams(vmem_limit_bytes=VMEM_LIMIT),
        cost_estimate=cost(8 * block_rows * slots * size**3, 2 * split_h.size),
        name="field",
    )(cols, coef, *operands)


GRAM_BLOCKS = 5


def gram_kernel(y_ref, own_ref, s_ref, u_ref, us_ref, o_ref, os_ref, out_ref, acc):
    step = pl.program_id(0)

    @pl.when(step == 0)
    def _():
        acc[...] = jnp.zeros_like(acc)

    lhs = jnp.concatenate(split(own_ref[...].T), axis=0)

    def add(block, ref):
        acc[block] += mm(lhs, jnp.concatenate(split(ref[...]), axis=1))

    for block, ref in enumerate((own_ref, s_ref, u_ref, us_ref)):
        add(block, ref)

    @pl.when(y_ref[0] < 2)
    def _():
        add(4, o_ref)

    @pl.when(y_ref[0] >= 2)
    def _():
        add(4, os_ref)

    @pl.when(step == pl.num_programs(0) - 1)
    def _():
        for block in range(GRAM_BLOCKS):
            out_ref[:, block * 128 : (block + 1) * 128] = fold(acc[block])


def gram_share(y, pieces):
    rows, cols = pieces[0].shape
    chunk = 512
    return pl.pallas_call(
        gram_kernel,
        out_shape=jax.ShapeDtypeStruct((cols, GRAM_BLOCKS * cols), F32),
        grid_spec=pltpu.PrefetchScalarGridSpec(
            num_scalar_prefetch=1,
            grid=(rows // chunk,),
            in_specs=[pl.BlockSpec((chunk, cols), lambda i, *_: (i, 0))] * len(pieces),
            out_specs=pl.BlockSpec((cols, GRAM_BLOCKS * cols), lambda i, *_: (0, 0)),
            scratch_shapes=[pltpu.VMEM((GRAM_BLOCKS, 2 * cols, 2 * cols), F32)],
        ),
        compiler_params=pltpu.CompilerParams(vmem_limit_bytes=VMEM_LIMIT),
        cost_estimate=cost(8 * rows * cols * cols * GRAM_BLOCKS, 4 * rows * cols * len(pieces)),
        name="gram_share",
    )(y, *pieces)


KEEP = {0: 1, 3: 2, 4: 1, 8: 1}
BASE = {2: 1, 6: 1, 10: 1, 11: 2}
PIECES = ((0, 0), (1, 0), (0, 1), (1, 1), (0, 3), (1, 3), (0, 2), (1, 2))


def finish_kernel(total_rows, y_ref, ga_ref, gb_ref, *rest):
    x_refs = rest[: len(PIECES)]
    out_ref, gram, gram_low, state, factor = rest[len(PIECES) :]
    grams = (ga_ref, gb_ref)
    y = y_ref[0]

    @pl.when(pl.program_id(0) == 0)
    def _():
        diagonal = lax.broadcasted_iota(jnp.int32, (128, 128), 0) == lax.broadcasted_iota(
            jnp.int32, (128, 128), 1
        )

        def block(k, row, b):
            return grams[k][:, row, :, b * 128 : (b + 1) * 128].reshape(128, 128)

        trace = jnp.zeros((128, 128), F32)
        for k in range(2):
            for row in range(4):
                trace += jnp.where(diagonal, block(k, row, 0), 0.0)
        energy = jnp.sum(jnp.sum(trace, axis=0, keepdims=True), axis=1, keepdims=True)
        square = NV / (4 * (energy + 1e-06))

        def put(at_row, at_col, value):
            high, low = split(value)
            rows, cols = slice(at_row * 128, at_row * 128 + 128), slice(at_col * 128, at_col * 128 + 128)
            gram[rows, cols] = high
            gram_low[rows, cols] = low

        for k in range(2):
            for row in range(4):
                here = 4 * k + row
                after, across = (row + 1) % 4, (row + 2) % 4
                side = k if row < 2 else 1 - k
                put(here, here, block(k, row, 0) * square)
                put(here, 4 * (1 - k) + row, block(k, row, 1) * square)
                for there, b in ((4 * k + after, 2), (4 * (1 - k) + after, 3), (4 * side + across, 4)):
                    value = block(k, row, b) * square
                    put(here, there, value)
                    put(there, here, value.T)

        mine = pl.ds(pl.multiple_of(y * 128, 128), 128)
        column = lax.broadcasted_iota(jnp.int32, (128, NV), 1) - y * 128
        unit = (column == lax.broadcasted_iota(jnp.int32, (128, NV), 0)).astype(F32)
        state[0] = 1.5 * unit - 0.5 * (gram[mine, :].astype(F32) + gram_low[mine, :].astype(F32))

        @pl.loop(0, 12)
        def _(step):
            current = state[0]
            for at, slot in KEEP.items():

                @pl.when(step == at)
                def _():
                    state[slot] = current

            slot = jnp.int32(0)
            for at, value in BASE.items():
                slot = jnp.where(step == at, value, slot)
            high, low = split(current)
            twice = mm(jnp.concatenate([high, low], axis=0), gram[...])
            product = (twice[:128] + twice[128:]) + mm(high, gram_low[...])
            state[0] = 1.5 * state[slot] - 0.5 * product

        scale = jnp.sqrt(square) * math.sqrt(total_rows)
        high, low = split(state[0].T * scale)
        factor[:, :128] = high
        factor[:, 128:] = low

    lhs = jnp.concatenate([ref[...] for ref in x_refs], axis=1)
    rhs = jnp.concatenate(
        [
            factor[pl.ds(pl.multiple_of((4 * k + lax.rem(y + dy, 4)) * 128, 128), 128), :]
            for k, dy in PIECES
        ],
        axis=0,
    )
    out_ref[...] = fold(mm(jnp.concatenate(split(lhs), axis=0), rhs))


def finish(total_rows, y, gram_a, gram_b, pieces):
    rows, cols = pieces[0].shape
    chunk = 256
    whole = pl.BlockSpec(gram_a.shape, lambda i, *_: (0, 0, 0, 0))
    part = pl.BlockSpec((chunk, cols), lambda i, *_: (i, 0))
    return pl.pallas_call(
        functools.partial(finish_kernel, total_rows),
        out_shape=jax.ShapeDtypeStruct((rows, cols), F32),
        grid_spec=pltpu.PrefetchScalarGridSpec(
            num_scalar_prefetch=1,
            grid=(rows // chunk,),
            in_specs=[whole, whole] + [part] * len(pieces),
            out_specs=part,
            scratch_shapes=[
                pltpu.VMEM((NV, NV), BF),
                pltpu.VMEM((NV, NV), BF),
                pltpu.VMEM((3, cols, NV), F32),
                pltpu.VMEM((NV, 2 * cols), BF),
            ],
        ),
        compiler_params=pltpu.CompilerParams(vmem_limit_bytes=VMEM_LIMIT),
        cost_estimate=cost(12 * 6 * cols * NV * NV, 4 * rows * cols * 9),
        name="finish",
    )(y, gram_a, gram_b, *pieces)


def on_device(vectors, hamiltonian, column_blocks, live_counts, lower_bound, upper_bound):
    rows_dev, panel_cols = vectors.shape
    block_rows, slot_count, block_size, unused_size = hamiltonian.shape
    row_count, vec_count = lax.axis_size("row"), lax.axis_size("vec")
    first_row = lax.axis_index("row") * block_rows
    local = (column_blocks - first_row + block_rows) % (block_rows * row_count)
    live = jnp.arange(slot_count, dtype=jnp.int32)[None, :] < live_counts[:, None]
    cols = jnp.where(live, jnp.minimum(local, 3 * block_rows - 1), 3 * block_rows).reshape(-1)
    centre = (upper_bound[0] + lower_bound[0]) / 2
    radius = (upper_bound[0] - lower_bound[0]) / 2
    coef = jnp.stack([centre, 1.0 / radius])
    y = (lax.axis_index("vec") // 2)[None].astype(jnp.int32)

    def from_row(value, step):
        return lax.ppermute(value, "row", [((i + step) % row_count, i) for i in range(row_count)])

    def from_y(value, step):
        return lax.ppermute(
            value, "vec", [((i + 2 * step) % vec_count, i) for i in range(vec_count)]
        )

    def swap(value):
        return lax.ppermute(value, "vec", [(i, i ^ 1) for i in range(vec_count)])

    split_h = split_blocks(hamiltonian)
    blocks = vectors.reshape(block_rows, block_size, panel_cols)
    first = apply_field(False, cols, coef, split_h, from_row(blocks, -1), blocks, from_row(blocks, 1))
    second = apply_field(
        True, cols, coef, split_h, from_row(first, -1), first, from_row(first, 1), blocks
    )
    own = second.reshape(rows_dev, panel_cols)

    half = rows_dev // 2
    up, down = from_y(own, 1), from_y(own, -1)
    across = jnp.concatenate([from_y(up[:half], 1), from_y(down[half:], -1)], axis=0)
    pieces = (own, swap(own), up, swap(up), down, swap(down), across, swap(across))

    share = gram_share(y, pieces[:4] + pieces[6:])
    strip = share.shape[0] // row_count
    parts = lax.all_to_all(
        share.reshape(row_count, strip, -1), "row", split_axis=0, concat_axis=0, tiled=True
    )
    part = jnp.sum(parts, axis=0)
    groups = [
        [r * vec_count + v for r in range(row_count) for v in range(core, vec_count, 2)]
        for core in range(2)
    ]
    members = row_count * vec_count // 2
    gram_a = lax.all_to_all(
        jnp.broadcast_to(part[None], (members,) + part.shape),
        ("row", "vec"),
        split_axis=0,
        concat_axis=0,
        tiled=True,
        axis_index_groups=groups,
    ).reshape(row_count, vec_count // 2, strip, -1)
    gram_b = swap(gram_a)
    return finish(rows_dev * row_count, y, gram_a, gram_b, pieces)


def solution(mesh):
    placed = (P("row", "vec"), P("row", None, None, None), P("row", None), P("row"), P(), P())
    return jax.shard_map(
        on_device, mesh=mesh, in_specs=placed, out_specs=P("row", "vec"), check_vma=False
    )
```

```python
import functools
import math

import jax
import jax.numpy as jnp
from jax import lax
from jax.experimental import pallas as pl
from jax.experimental.pallas import tpu as pltpu
from jax.sharding import PartitionSpec as P

NV = 1024
BF = jnp.bfloat16
F32 = jnp.float32
VMEM_LIMIT = 56 * 1024 * 1024


def split(x):
    high = x.astype(BF)
    return high, (x - high.astype(F32)).astype(BF)


def fold(full):
    rows, cols = full.shape[0] // 2, full.shape[1] // 2
    return (full[:rows, :cols] + full[rows:, :cols]) + (full[:rows, cols:] + full[rows:, cols:])


def mm(a, b):
    return jnp.dot(a, b, preferred_element_type=F32)


def cost(flops, moved):
    return pl.CostEstimate(flops=flops, bytes_accessed=moved, transcendentals=0)


def split_kernel(h_ref, o_ref):
    high, low = split(h_ref[0])
    o_ref[0, :, :128, :] = high
    o_ref[0, :, 128:, :] = low


def split_blocks(hamiltonian):
    block_rows, slots, size, _ = hamiltonian.shape
    return pl.pallas_call(
        split_kernel,
        out_shape=jax.ShapeDtypeStruct((block_rows, slots, 2 * size, size), BF),
        grid=(block_rows,),
        in_specs=[pl.BlockSpec((1, slots, size, size), lambda i: (i, 0, 0, 0))],
        out_specs=pl.BlockSpec((1, slots, 2 * size, size), lambda i: (i, 0, 0, 0)),
        compiler_params=pltpu.CompilerParams(vmem_limit_bytes=VMEM_LIMIT),
        cost_estimate=cost(0, 8 * block_rows * slots * size * size),
        name="split_blocks",
    )(hamiltonian)


SMEM_SPEC = pl.BlockSpec(memory_space=pltpu.SMEM)
VMEM_SPEC = pl.BlockSpec(memory_space=pltpu.VMEM)


def field_kernel(second, cols_ref, coef_ref, h_ref, left_ref, own_ref, right_ref, *rest):
    if second:
        prev_ref, o_ref, wide = rest
    else:
        o_ref, wide = rest
    count, slots = h_ref.shape[:2]
    for part, ref in enumerate((left_ref, own_ref, right_ref)):

        @pl.loop(0, count)
        def _(j):
            high, low = split(ref[j])
            wide[part * count + j, :, :128] = high
            wide[part * count + j, :, 128:] = low

    wide[3 * count] = jnp.zeros(wide.shape[1:], BF)
    centre, inverse = coef_ref[0], coef_ref[1]

    @pl.loop(0, count)
    def _(i):
        lhs = jnp.concatenate([h_ref[i, k] for k in range(slots)], axis=1)
        rhs = jnp.concatenate([wide[cols_ref[i * slots + k]] for k in range(slots)], axis=0)
        result = (fold(mm(lhs, rhs)) - centre * own_ref[i]) * inverse
        if second:
            result = 2.0 * result - prev_ref[i]
        o_ref[i] = result


def apply_field(second, cols, coef, split_h, left, own, right, prev=None):
    block_rows, slots, double, size = split_h.shape
    operands = [split_h, left, own, right] + ([prev] if second else [])
    return pl.pallas_call(
        functools.partial(field_kernel, second),
        out_shape=jax.ShapeDtypeStruct((block_rows, size, size), F32),
        in_specs=[SMEM_SPEC] * 2 + [VMEM_SPEC] * len(operands),
        out_specs=VMEM_SPEC,
        scratch_shapes=[pltpu.VMEM((3 * block_rows + 1, size, 2 * size), BF)],
        compiler_params=pltpu.CompilerParams(vmem_limit_bytes=30 * 2**20),
        cost_estimate=cost(8 * block_rows * slots * size**3, 2 * split_h.size),
        name="field",
    )(cols, coef, *operands)


GRAM_BLOCKS = 5


def gram_kernel(y_ref, own_ref, s_ref, u_ref, us_ref, d_ref, out_ref, acc):
    acc[...] = jnp.zeros_like(acc)
    chunk = 512

    @pl.loop(0, own_ref.shape[0] // chunk)
    def _(step):
        rows = pl.ds(pl.multiple_of(step * chunk, chunk), chunk)

        def turned(ref):
            return jnp.concatenate(split(ref[rows, :].T), axis=0)

        def paired(ref):
            return jnp.concatenate(split(ref[rows, :]), axis=1)

        lhs = turned(own_ref)
        for block, ref in enumerate((own_ref, s_ref, u_ref, us_ref)):
            acc[block] += mm(lhs, paired(ref))
        lhs = turned(d_ref)

        @pl.when(y_ref[0] < 2)
        def _():
            acc[4] += mm(lhs, paired(u_ref))

        @pl.when(y_ref[0] >= 2)
        def _():
            acc[4] += mm(lhs, paired(us_ref))

    for block in range(GRAM_BLOCKS):
        out_ref[:, block * 128 : (block + 1) * 128] = fold(acc[block])


def gram_share(y, pieces):
    rows, cols = pieces[0].shape
    return pl.pallas_call(
        gram_kernel,
        out_shape=jax.ShapeDtypeStruct((cols, GRAM_BLOCKS * cols), F32),
        in_specs=[SMEM_SPEC] + [VMEM_SPEC] * len(pieces),
        out_specs=VMEM_SPEC,
        scratch_shapes=[pltpu.VMEM((GRAM_BLOCKS, 2 * cols, 2 * cols), F32)],
        compiler_params=pltpu.CompilerParams(vmem_limit_bytes=30 * 2**20),
        cost_estimate=cost(8 * rows * cols * cols * GRAM_BLOCKS, 4 * rows * cols * len(pieces)),
        name="gram_share",
    )(y, *pieces)


KEEP = {0: 1, 3: 2, 4: 1, 8: 1}
BASE = {2: 1, 6: 1, 10: 1, 11: 2}
PIECES = ((0, 0), (1, 0), (0, 1), (1, 1), (0, 3), (1, 3), (0, 2), (1, 2))


def finish_kernel(total_rows, y_ref, ga_ref, gb_ref, *rest):
    x_refs = rest[: len(PIECES)]
    out_ref, gram, gram_low, state, factor, ordered = rest[len(PIECES) :]
    grams = (ga_ref, gb_ref)
    y = y_ref[0]

    if True:
        diagonal = lax.broadcasted_iota(jnp.int32, (128, 128), 0) == lax.broadcasted_iota(
            jnp.int32, (128, 128), 1
        )

        def block(k, row, b):
            return grams[k][:, row, :, b * 128 : (b + 1) * 128].reshape(128, 128)

        trace = jnp.zeros((128, 128), F32)
        for k in range(2):
            for row in range(4):
                trace += jnp.where(diagonal, block(k, row, 0), 0.0)
        energy = jnp.sum(jnp.sum(trace, axis=0, keepdims=True), axis=1, keepdims=True)
        square = NV / (4 * (energy + 1e-06))

        def put(at_row, at_col, value):
            high, low = split(value)
            rows, cols = slice(at_row * 128, at_row * 128 + 128), slice(at_col * 128, at_col * 128 + 128)
            gram[rows, cols] = high
            gram_low[rows, cols] = low

        for k in range(2):
            for row in range(4):
                here = 4 * k + row
                after, before = (row + 1) % 4, (row + 3) % 4
                side = k if row < 2 else 1 - k
                put(here, here, block(k, row, 0) * square)
                put(here, 4 * (1 - k) + row, block(k, row, 1) * square)
                for one, two, b in (
                    (here, 4 * k + after, 2),
                    (here, 4 * (1 - k) + after, 3),
                    (4 * k + before, 4 * side + after, 4),
                ):
                    value = block(k, row, b) * square
                    put(one, two, value)
                    put(two, one, value.T)

        mine = pl.ds(pl.multiple_of(y * 128, 128), 128)
        column = lax.broadcasted_iota(jnp.int32, (128, NV), 1) - y * 128
        unit = (column == lax.broadcasted_iota(jnp.int32, (128, NV), 0)).astype(F32)
        state[0] = 1.5 * unit - 0.5 * (gram[mine, :].astype(F32) + gram_low[mine, :].astype(F32))

        @pl.loop(0, 12)
        def _(step):
            current = state[0]
            for at, slot in KEEP.items():

                @pl.when(step == at)
                def _():
                    state[slot] = current

            slot = jnp.int32(0)
            for at, value in BASE.items():
                slot = jnp.where(step == at, value, slot)
            high, low = split(current)
            twice = mm(jnp.concatenate([high, low], axis=0), gram[...])
            product = (twice[:128] + twice[128:]) + mm(high, gram_low[...])
            state[0] = 1.5 * state[slot] - 0.5 * product

        scale = jnp.sqrt(square) * math.sqrt(total_rows)
        high, low = split(state[0].T * scale)
        factor[:, :128] = high
        factor[:, 128:] = low

    rhs = jnp.concatenate(
        [
            factor[pl.ds(pl.multiple_of((4 * k + lax.rem(y + dy, 4)) * 128, 128), 128), :]
            for k, dy in PIECES
        ],
        axis=0,
    )
    ordered[...] = rhs
    chunk = 256

    @pl.loop(0, out_ref.shape[0] // chunk)
    def _(step):
        rows = pl.ds(pl.multiple_of(step * chunk, chunk), chunk)
        lhs = jnp.concatenate([ref[rows, :] for ref in x_refs], axis=1)
        out_ref[rows, :] = fold(mm(jnp.concatenate(split(lhs), axis=0), ordered[...]))


def finish(total_rows, y, gram_a, gram_b, pieces):
    rows, cols = pieces[0].shape
    return pl.pallas_call(
        functools.partial(finish_kernel, total_rows),
        out_shape=jax.ShapeDtypeStruct((rows, cols), F32),
        in_specs=[SMEM_SPEC] + [VMEM_SPEC] * (2 + len(pieces)),
        out_specs=VMEM_SPEC,
        scratch_shapes=[
            pltpu.VMEM((NV, NV), BF),
            pltpu.VMEM((NV, NV), BF),
            pltpu.VMEM((3, cols, NV), F32),
            pltpu.VMEM((NV, 2 * cols), BF),
            pltpu.VMEM((NV, 2 * cols), BF),
        ],
        compiler_params=pltpu.CompilerParams(vmem_limit_bytes=40 * 2**20),
        cost_estimate=cost(12 * 6 * cols * NV * NV, 4 * rows * cols * 9),
        name="finish",
    )(y, gram_a, gram_b, *pieces)


def on_device(vectors, hamiltonian, column_blocks, live_counts, lower_bound, upper_bound):
    rows_dev, panel_cols = vectors.shape
    block_rows, slot_count, block_size, unused_size = hamiltonian.shape
    row_count, vec_count = lax.axis_size("row"), lax.axis_size("vec")
    first_row = lax.axis_index("row") * block_rows
    local = (column_blocks - first_row + block_rows) % (block_rows * row_count)
    live = jnp.arange(slot_count, dtype=jnp.int32)[None, :] < live_counts[:, None]
    cols = jnp.where(live, jnp.minimum(local, 3 * block_rows - 1), 3 * block_rows).reshape(-1)
    centre = (upper_bound[0] + lower_bound[0]) / 2
    radius = (upper_bound[0] - lower_bound[0]) / 2
    coef = jnp.stack([centre, 1.0 / radius])
    y = (lax.axis_index("vec") // 2)[None].astype(jnp.int32)

    def from_row(value, step):
        return lax.ppermute(value, "row", [((i + step) % row_count, i) for i in range(row_count)])

    def from_y(value, step):
        return lax.ppermute(
            value, "vec", [((i + 2 * step) % vec_count, i) for i in range(vec_count)]
        )

    def swap(value):
        return lax.ppermute(value, "vec", [(i, i ^ 1) for i in range(vec_count)])

    split_h = split_blocks(hamiltonian)
    blocks = vectors.reshape(block_rows, block_size, panel_cols)
    first = apply_field(False, cols, coef, split_h, from_row(blocks, -1), blocks, from_row(blocks, 1))
    second = apply_field(
        True, cols, coef, split_h, from_row(first, -1), first, from_row(first, 1), blocks
    )
    own = second.reshape(rows_dev, panel_cols)

    half = rows_dev // 2
    up, down = from_y(own, 1), from_y(own, -1)
    across = jnp.concatenate([from_y(up[:half], 1), from_y(down[half:], -1)], axis=0)
    pieces = (own, swap(own), up, swap(up), down, swap(down), across, swap(across))

    share = gram_share(y, pieces[:5])
    strip = share.shape[0] // row_count
    parts = lax.all_to_all(
        share.reshape(row_count, strip, -1), "row", split_axis=0, concat_axis=0, tiled=True
    )
    part = jnp.sum(parts, axis=0)
    groups = [
        [r * vec_count + v for r in range(row_count) for v in range(core, vec_count, 2)]
        for core in range(2)
    ]
    members = row_count * vec_count // 2
    gram_a = lax.all_to_all(
        jnp.broadcast_to(part[None], (members,) + part.shape),
        ("row", "vec"),
        split_axis=0,
        concat_axis=0,
        tiled=True,
        axis_index_groups=groups,
    ).reshape(row_count, vec_count // 2, strip, -1)
    gram_b = swap(gram_a)
    return finish(rows_dev * row_count, y, gram_a, gram_b, pieces)


def solution(mesh):
    placed = (P("row", "vec"), P("row", None, None, None), P("row", None), P("row"), P(), P())
    return jax.shard_map(
        on_device, mesh=mesh, in_specs=placed, out_specs=P("row", "vec"), check_vma=False
    )
```

```python
import functools
import math

import jax
import jax.numpy as jnp
from jax import lax
from jax.experimental import pallas as pl
from jax.experimental.pallas import tpu as pltpu
from jax.sharding import PartitionSpec as P


NV = 1024
BF = jnp.bfloat16
F32 = jnp.float32


def split(x):
    high = x.astype(BF)
    return high, (x - high.astype(F32)).astype(BF)


def fold(full):
    rows, cols = full.shape[0] // 2, full.shape[1] // 2
    return (full[:rows, :cols] + full[rows:, :cols]) + (full[:rows, cols:] + full[rows:, cols:])


def mm(a, b):
    return jnp.dot(a, b, preferred_element_type=F32)


def cost(flops, moved):
    return pl.CostEstimate(flops=flops, bytes_accessed=moved, transcendentals=0)


DEPTH = 4


def split_kernel(h_ref, o_ref, buffer, arrived):
    count, size = o_ref.shape[0], h_ref.shape[-1]

    def fetch(row, slot):
        return pltpu.make_async_copy(h_ref.at[row], buffer.at[slot], arrived.at[slot])

    for slot in range(DEPTH):
        fetch(slot, slot).start()

    @pl.loop(0, count)
    def _(row):
        slot = lax.rem(row, DEPTH)
        fetch(row, slot).wait()

        @pl.loop(0, o_ref.shape[1])
        def _(k):
            high, low = split(buffer[slot, k])
            o_ref[row, k, :size, :] = high
            o_ref[row, k, size:, :] = low

        @pl.when(row + DEPTH < count)
        def _():
            fetch(row + DEPTH, slot).start()


def split_blocks(hamiltonian):
    block_rows, slots, size, _ = hamiltonian.shape
    return pl.pallas_call(
        split_kernel,
        out_shape=jax.ShapeDtypeStruct((block_rows, slots, 2 * size, size), BF),
        in_specs=[pl.BlockSpec(memory_space=pl.ANY)],
        out_specs=pl.BlockSpec(memory_space=pltpu.VMEM),
        scratch_shapes=[
            pltpu.VMEM((DEPTH, slots, size, size), F32),
            pltpu.SemaphoreType.DMA((DEPTH,)),
        ],
        compiler_params=pltpu.CompilerParams(vmem_limit_bytes=30 * 2**20),
        cost_estimate=cost(0, 8 * block_rows * slots * size * size),
        name="split_blocks",
    )(hamiltonian)


SMEM_SPEC = pl.BlockSpec(memory_space=pltpu.SMEM)
VMEM_SPEC = pl.BlockSpec(memory_space=pltpu.VMEM)


def field_kernel(second, cols_ref, coef_ref, h_ref, left_ref, own_ref, right_ref, *rest):
    if second:
        prev_ref, o_ref, wide = rest
    else:
        o_ref, wide = rest
    count, slots = h_ref.shape[:2]
    for part, ref in enumerate((left_ref, own_ref, right_ref)):

        @pl.loop(0, count)
        def _(j):
            high, low = split(ref[j])
            wide[part * count + j, :, :128] = high
            wide[part * count + j, :, 128:] = low

    wide[3 * count] = jnp.zeros(wide.shape[1:], BF)
    centre, inverse = coef_ref[0], coef_ref[1]

    @pl.loop(0, count)
    def _(i):
        lhs = jnp.concatenate([h_ref[i, k] for k in range(slots)], axis=1)
        rhs = jnp.concatenate([wide[cols_ref[i * slots + k]] for k in range(slots)], axis=0)
        result = (fold(mm(lhs, rhs)) - centre * own_ref[i]) * inverse
        if second:
            result = 2.0 * result - prev_ref[i]
        o_ref[i] = result


def apply_field(second, cols, coef, split_h, left, own, right, prev=None):
    block_rows, slots, _, size = split_h.shape
    operands = [split_h, left, own, right] + ([prev] if second else [])
    return pl.pallas_call(
        functools.partial(field_kernel, second),
        out_shape=jax.ShapeDtypeStruct((block_rows, size, size), F32),
        in_specs=[SMEM_SPEC] * 2 + [VMEM_SPEC] * len(operands),
        out_specs=VMEM_SPEC,
        scratch_shapes=[pltpu.VMEM((3 * block_rows + 1, size, 2 * size), BF)],
        compiler_params=pltpu.CompilerParams(vmem_limit_bytes=30 * 2**20),
        cost_estimate=cost(8 * block_rows * slots * size**3, 2 * split_h.size),
        name="field",
    )(cols, coef, *operands)


GRAM_BLOCKS = 5


def gram_kernel(y_ref, own_ref, s_ref, u_ref, us_ref, d_ref, out_ref, acc):
    acc[...] = jnp.zeros_like(acc)
    chunk = 512

    @pl.loop(0, own_ref.shape[0] // chunk)
    def _(step):
        rows = pl.ds(pl.multiple_of(step * chunk, chunk), chunk)

        def turned(ref):
            return jnp.concatenate(split(ref[rows, :].T), axis=0)

        def paired(ref):
            return jnp.concatenate(split(ref[rows, :]), axis=1)

        lhs = turned(own_ref)
        for block, ref in enumerate((own_ref, s_ref, u_ref, us_ref)):
            acc[block] += mm(lhs, paired(ref))
        lhs = turned(d_ref)

        @pl.when(y_ref[0] < 2)
        def _():
            acc[4] += mm(lhs, paired(u_ref))

        @pl.when(y_ref[0] >= 2)
        def _():
            acc[4] += mm(lhs, paired(us_ref))

    for block in range(GRAM_BLOCKS):
        out_ref[:, block * 128 : (block + 1) * 128] = fold(acc[block])


def gram_share(y, pieces):
    rows, cols = pieces[0].shape
    return pl.pallas_call(
        gram_kernel,
        out_shape=jax.ShapeDtypeStruct((cols, GRAM_BLOCKS * cols), F32),
        in_specs=[SMEM_SPEC] + [VMEM_SPEC] * len(pieces),
        out_specs=VMEM_SPEC,
        scratch_shapes=[pltpu.VMEM((GRAM_BLOCKS, 2 * cols, 2 * cols), F32)],
        compiler_params=pltpu.CompilerParams(vmem_limit_bytes=30 * 2**20),
        cost_estimate=cost(8 * rows * cols * cols * GRAM_BLOCKS, 4 * rows * cols * len(pieces)),
        name="gram_share",
    )(y, *pieces)


KEEP = {0: 1, 3: 2, 4: 1, 8: 1}
BASE = {2: 1, 6: 1, 10: 1, 11: 2}
PIECES = ((0, 0), (1, 0), (0, 1), (1, 1), (0, 3), (1, 3), (0, 2), (1, 2))
WHOLE = 6


def finish_kernel(total_rows, y_ref, ga_ref, gb_ref, *rest):
    x_refs = rest[:WHOLE]
    halves = (rest[WHOLE : WHOLE + 2], rest[WHOLE + 2 : WHOLE + 4])
    out_ref, gram, gram_low, state, factor, ordered = rest[WHOLE + 4 :]
    grams = (ga_ref, gb_ref)
    y = y_ref[0]

    diagonal = lax.broadcasted_iota(jnp.int32, (128, 128), 0) == lax.broadcasted_iota(
        jnp.int32, (128, 128), 1
    )

    def block(k, row, b):
        return grams[k][:, row, :, b * 128 : (b + 1) * 128].reshape(128, 128)

    trace = jnp.zeros((128, 128), F32)
    for k in range(2):
        for row in range(4):
            trace += jnp.where(diagonal, block(k, row, 0), 0.0)
    energy = jnp.sum(jnp.sum(trace, axis=0, keepdims=True), axis=1, keepdims=True)
    square = NV / (4 * (energy + 1e-06))

    def put(at_row, at_col, value):
        high, low = split(value)
        rows, cols = slice(at_row * 128, at_row * 128 + 128), slice(at_col * 128, at_col * 128 + 128)
        gram[rows, cols] = high
        gram_low[rows, cols] = low

    for k in range(2):
        for row in range(4):
            here = 4 * k + row
            after, before = (row + 1) % 4, (row + 3) % 4
            side = k if row < 2 else 1 - k
            put(here, here, block(k, row, 0) * square)
            put(here, 4 * (1 - k) + row, block(k, row, 1) * square)
            for one, two, b in (
                (here, 4 * k + after, 2),
                (here, 4 * (1 - k) + after, 3),
                (4 * k + before, 4 * side + after, 4),
            ):
                value = block(k, row, b) * square
                put(one, two, value)
                put(two, one, value.T)

    mine = pl.ds(pl.multiple_of(y * 128, 128), 128)
    column = lax.broadcasted_iota(jnp.int32, (128, NV), 1) - y * 128
    unit = (column == lax.broadcasted_iota(jnp.int32, (128, NV), 0)).astype(F32)
    state[0] = 1.5 * unit - 0.5 * (gram[mine, :].astype(F32) + gram_low[mine, :].astype(F32))

    @pl.loop(0, 12)
    def _(step):
        current = state[0]
        for at, slot in KEEP.items():

            @pl.when(step == at)
            def _():
                state[slot] = current

        slot = jnp.int32(0)
        for at, value in BASE.items():
            slot = jnp.where(step == at, value, slot)
        high, low = split(current)
        twice = mm(jnp.concatenate([high, low], axis=0), gram[...])
        product = (twice[:128] + twice[128:]) + mm(high, gram_low[...])
        state[0] = 1.5 * state[slot] - 0.5 * product

    scale = jnp.sqrt(square) * math.sqrt(total_rows)
    high, low = split(state[0].T * scale)
    factor[:, :128] = high
    factor[:, 128:] = low

    rhs = jnp.concatenate(
        [
            factor[pl.ds(pl.multiple_of((4 * k + lax.rem(y + dy, 4)) * 128, 128), 128), :]
            for k, dy in PIECES
        ],
        axis=0,
    )
    ordered[...] = rhs
    chunk = 256
    half = out_ref.shape[0] // 2
    for part in range(2):

        @pl.loop(0, half // chunk)
        def _(step):
            within = pl.ds(pl.multiple_of(step * chunk, chunk), chunk)
            rows = pl.ds(pl.multiple_of(part * half + step * chunk, chunk), chunk)
            parts = [ref[rows, :] for ref in x_refs] + [ref[part][within, :] for ref in halves]
            lhs = jnp.concatenate(split(jnp.concatenate(parts, axis=1)), axis=0)
            out_ref[rows, :] = fold(mm(lhs, ordered[...]))


def finish(total_rows, y, gram_a, gram_b, pieces):
    rows, cols = pieces[0].shape
    return pl.pallas_call(
        functools.partial(finish_kernel, total_rows),
        out_shape=jax.ShapeDtypeStruct((rows, cols), F32),
        in_specs=[SMEM_SPEC] + [VMEM_SPEC] * (2 + len(pieces)),
        out_specs=VMEM_SPEC,
        scratch_shapes=[
            pltpu.VMEM((NV, NV), BF),
            pltpu.VMEM((NV, NV), BF),
            pltpu.VMEM((3, cols, NV), F32),
            pltpu.VMEM((NV, 2 * cols), BF),
            pltpu.VMEM((NV, 2 * cols), BF),
        ],
        compiler_params=pltpu.CompilerParams(vmem_limit_bytes=40 * 2**20),
        cost_estimate=cost(12 * 6 * cols * NV * NV, 4 * rows * cols * 9),
        name="finish",
    )(y, gram_a, gram_b, *pieces)


def on_device(vectors, hamiltonian, column_blocks, live_counts, lower_bound, upper_bound):
    rows_dev, panel_cols = vectors.shape
    block_rows, slot_count, block_size, _ = hamiltonian.shape
    row_count, vec_count = lax.axis_size("row"), lax.axis_size("vec")
    first_row = lax.axis_index("row") * block_rows
    local = (column_blocks - first_row + block_rows) % (block_rows * row_count)
    live = jnp.arange(slot_count, dtype=jnp.int32)[None, :] < live_counts[:, None]
    cols = jnp.where(live, jnp.minimum(local, 3 * block_rows - 1), 3 * block_rows).reshape(-1)
    centre = (upper_bound[0] + lower_bound[0]) / 2
    radius = (upper_bound[0] - lower_bound[0]) / 2
    coef = jnp.stack([centre, 1.0 / radius])
    y = (lax.axis_index("vec") // 2)[None].astype(jnp.int32)

    def from_row(value, step):
        return lax.ppermute(value, "row", [((i + step) % row_count, i) for i in range(row_count)])

    def from_y(value, step):
        return lax.ppermute(
            value, "vec", [((i + 2 * step) % vec_count, i) for i in range(vec_count)]
        )

    def swap(value):
        return lax.ppermute(value, "vec", [(i, i ^ 1) for i in range(vec_count)])

    split_h = split_blocks(hamiltonian)
    blocks = vectors.reshape(block_rows, block_size, panel_cols)
    first = apply_field(False, cols, coef, split_h, from_row(blocks, -1), blocks, from_row(blocks, 1))
    second = apply_field(
        True, cols, coef, split_h, from_row(first, -1), first, from_row(first, 1), blocks
    )
    own = second.reshape(rows_dev, panel_cols)

    half = rows_dev // 2
    up = from_y(own, 1)
    down = from_y(own, -1)
    own_s = swap(own)
    up_s = swap(up)
    down_s = swap(down)
    across, across_s = [], []
    for part, source, step in ((0, up[:half], 1), (1, down[half:], -1)):
        across.append(from_y(source, step))
        across_s.append(swap(across[-1]))
    share = gram_share(y, (own, own_s, up, up_s, down))
    strip = share.shape[0] // row_count
    parts = lax.all_to_all(
        share.reshape(row_count, strip, -1), "row", split_axis=0, concat_axis=0, tiled=True
    )
    part = jnp.sum(parts, axis=0)
    groups = [
        [r * vec_count + v for r in range(row_count) for v in range(core, vec_count, 2)]
        for core in range(2)
    ]
    members = row_count * vec_count // 2
    gram_a = lax.all_to_all(
        jnp.broadcast_to(part[None], (members,) + part.shape),
        ("row", "vec"),
        split_axis=0,
        concat_axis=0,
        tiled=True,
        axis_index_groups=groups,
    ).reshape(row_count, vec_count // 2, strip, -1)
    gram_b = swap(gram_a)
    pieces = (own, own_s, up, up_s, down, down_s, *across, *across_s)
    return finish(rows_dev * row_count, y, gram_a, gram_b, pieces)


def solution(mesh):
    placed = (P("row", "vec"), P("row", None, None, None), P("row", None), P("row"), P(), P())

    return jax.shard_map(
        on_device, mesh=mesh, in_specs=placed, out_specs=P("row", "vec"), check_vma=False
    )
```

```python
import functools
import math

import jax
import jax.numpy as jnp
from jax import lax
from jax.experimental import pallas as pl
from jax.experimental.pallas import tpu as pltpu
from jax.sharding import PartitionSpec as P


NV = 1024
BF = jnp.bfloat16
F32 = jnp.float32


def split(x):
    high = x.astype(BF)
    return high, (x - high.astype(F32)).astype(BF)


def fold(full):
    rows, cols = full.shape[0] // 2, full.shape[1] // 2
    return (full[:rows, :cols] + full[rows:, :cols]) + (full[:rows, cols:] + full[rows:, cols:])


def mm(a, b):
    return jnp.dot(a, b, preferred_element_type=F32)


def cost(flops, moved):
    return pl.CostEstimate(flops=flops, bytes_accessed=moved, transcendentals=0)


DEPTH = 4


def split_kernel(h_ref, o_ref, buffer, arrived):
    count, size = o_ref.shape[0], h_ref.shape[-1]

    def fetch(row, slot):
        return pltpu.make_async_copy(h_ref.at[row], buffer.at[slot], arrived.at[slot])

    for slot in range(DEPTH):
        fetch(slot, slot).start()

    @pl.loop(0, count)
    def _(row):
        slot = lax.rem(row, DEPTH)
        fetch(row, slot).wait()

        @pl.loop(0, o_ref.shape[1])
        def _(k):
            high, low = split(buffer[slot, k])
            o_ref[row, k, :size, :] = high
            o_ref[row, k, size:, :] = low

        @pl.when(row + DEPTH < count)
        def _():
            fetch(row + DEPTH, slot).start()


def split_blocks(hamiltonian):
    block_rows, slots, size, _ = hamiltonian.shape
    return pl.pallas_call(
        split_kernel,
        out_shape=jax.ShapeDtypeStruct((block_rows, slots, 2 * size, size), BF),
        in_specs=[pl.BlockSpec(memory_space=pl.ANY)],
        out_specs=pl.BlockSpec(memory_space=pltpu.VMEM),
        scratch_shapes=[
            pltpu.VMEM((DEPTH, slots, size, size), F32),
            pltpu.SemaphoreType.DMA((DEPTH,)),
        ],
        compiler_params=pltpu.CompilerParams(vmem_limit_bytes=30 * 2**20),
        cost_estimate=cost(0, 8 * block_rows * slots * size * size),
        name="split_blocks",
    )(hamiltonian)


SMEM_SPEC = pl.BlockSpec(memory_space=pltpu.SMEM)
VMEM_SPEC = pl.BlockSpec(memory_space=pltpu.VMEM)


CHUNKS = 2


def lanes_low(shape):
    return lax.broadcasted_iota(jnp.int32, shape, 1) < shape[1] // 2


def turn(x):
    return pltpu.roll(x, x.shape[1] // 2, 1)


def pack_kernel(v_ref, a_ref, b_ref):
    low = lanes_low(v_ref.shape[1:])
    half = a_ref.shape[0]

    @pl.loop(0, half)
    def _(j):
        one, two = v_ref[j], v_ref[j + half]
        a_ref[j] = jnp.where(low, one, turn(two))
        b_ref[j] = jnp.where(low, turn(one), two)


def pack(blocks):
    count, size, cols = blocks.shape
    shape = jax.ShapeDtypeStruct((count // 2, size, cols), F32)
    return pl.pallas_call(
        pack_kernel,
        out_shape=(shape, shape),
        in_specs=[VMEM_SPEC],
        out_specs=(VMEM_SPEC, VMEM_SPEC),
        compiler_params=pltpu.CompilerParams(vmem_limit_bytes=30 * 2**20),
        cost_estimate=cost(0, 8 * blocks.size),
        name="pack",
    )(blocks)


def field_kernel(second, cols_ref, coef_ref, h_ref, left_ref, own_ref, right_ref, *rest):
    if second:
        prev_ref, o_ref, wide = rest
    else:
        o_ref, wide = rest
    count, slots = h_ref.shape[:2]
    half = count // 2
    low = lanes_low(own_ref.shape[1:])
    for part, ref in enumerate((left_ref, own_ref, right_ref)):

        @pl.loop(0, half)
        def _(j):
            value = ref[j]
            high = value.astype(BF).astype(F32)
            rest_of = value - high
            wide[part * count + j] = jnp.where(low, high, turn(rest_of)).astype(BF)
            wide[part * count + half + j] = jnp.where(low, turn(high), rest_of).astype(BF)

    wide[3 * count] = jnp.zeros(wide.shape[1:], BF)
    centre, inverse = coef_ref[0], coef_ref[1]

    def row(i):
        lhs = jnp.concatenate([h_ref[i, k] for k in range(slots)], axis=1)
        rhs = jnp.concatenate([wide[cols_ref[i * slots + k]] for k in range(slots)], axis=0)
        full = mm(lhs, rhs)
        full = full[: full.shape[0] // 2] + full[full.shape[0] // 2 :]
        return full + turn(full)

    @pl.loop(0, half)
    def _(i):
        summed = jnp.where(low, row(i), row(i + half))
        result = (summed - centre * own_ref[i]) * inverse
        if second:
            result = 2.0 * result - prev_ref[i]
        o_ref[i] = result


def apply_field(second, cols, coef, split_h, left, own, right, prev=None):
    block_rows, slots, _, size = split_h.shape
    operands = [split_h, left, own, right] + ([prev] if second else [])
    return pl.pallas_call(
        functools.partial(field_kernel, second),
        out_shape=jax.ShapeDtypeStruct(own.shape, F32),
        in_specs=[SMEM_SPEC] * 2 + [VMEM_SPEC] * len(operands),
        out_specs=VMEM_SPEC,
        scratch_shapes=[pltpu.VMEM((3 * block_rows + 1, size, size), BF)],
        compiler_params=pltpu.CompilerParams(vmem_limit_bytes=30 * 2**20),
        cost_estimate=cost(8 * block_rows * slots * size**3, 2 * split_h.size),
        name="field",
    )(cols, coef, *operands)


def natural(refs, rows, part):
    a, b = (ref[rows, :] for ref in refs)
    low = lanes_low(a.shape)
    return jnp.where(low, turn(a), b) if part else jnp.where(low, a, turn(b))


GRAM_BLOCKS = 5


def gram_kernel(y_ref, *rest):
    own, beside, up, up_s, down = (rest[2 * n : 2 * n + 2] for n in range(5))
    out_ref, acc = rest[10:]
    acc[...] = jnp.zeros_like(acc)
    chunk = 512
    for part in range(2):

        @pl.loop(0, own[0].shape[0] // chunk)
        def _(step):
            rows = pl.ds(pl.multiple_of(step * chunk, chunk), chunk)

            def turned(refs):
                return jnp.concatenate(split(natural(refs, rows, part).T), axis=0)

            def paired(refs):
                return jnp.concatenate(split(natural(refs, rows, part)), axis=1)

            lhs = turned(own)
            for block, refs in enumerate((own, beside, up, up_s)):
                acc[block] += mm(lhs, paired(refs))
            lhs = turned(down)

            @pl.when(y_ref[0] < 2)
            def _():
                acc[4] += mm(lhs, paired(up))

            @pl.when(y_ref[0] >= 2)
            def _():
                acc[4] += mm(lhs, paired(up_s))

    for block in range(GRAM_BLOCKS):
        out_ref[:, block * 128 : (block + 1) * 128] = fold(acc[block])


def gram_share(y, pieces):
    operands = [chunk for piece in pieces for chunk in piece]
    rows, cols = operands[0].shape
    return pl.pallas_call(
        gram_kernel,
        out_shape=jax.ShapeDtypeStruct((cols, GRAM_BLOCKS * cols), F32),
        in_specs=[SMEM_SPEC] + [VMEM_SPEC] * len(operands),
        out_specs=VMEM_SPEC,
        scratch_shapes=[pltpu.VMEM((GRAM_BLOCKS, 2 * cols, 2 * cols), F32)],
        compiler_params=pltpu.CompilerParams(vmem_limit_bytes=30 * 2**20),
        cost_estimate=cost(16 * rows * cols * cols * GRAM_BLOCKS, 4 * rows * cols * len(operands)),
        name="gram_share",
    )(y, *operands)


KEEP = {0: 1, 3: 2, 4: 1, 8: 1}
BASE = {2: 1, 6: 1, 10: 1, 11: 2}
PIECES = ((0, 0), (1, 0), (0, 1), (1, 1), (0, 3), (1, 3), (0, 2), (1, 2))


def finish_kernel(total_rows, y_ref, ga_ref, gb_ref, *rest):
    x_refs = [rest[2 * n : 2 * n + 2] for n in range(len(PIECES))]
    out_ref, gram, gram_low, state, factor, ordered = rest[2 * len(PIECES) :]
    grams = (ga_ref, gb_ref)
    y = y_ref[0]

    diagonal = lax.broadcasted_iota(jnp.int32, (128, 128), 0) == lax.broadcasted_iota(
        jnp.int32, (128, 128), 1
    )

    def block(k, row, b):
        return grams[k][:, row, :, b * 128 : (b + 1) * 128].reshape(128, 128)

    trace = jnp.zeros((128, 128), F32)
    for k in range(2):
        for row in range(4):
            trace += jnp.where(diagonal, block(k, row, 0), 0.0)
    energy = jnp.sum(jnp.sum(trace, axis=0, keepdims=True), axis=1, keepdims=True)
    square = NV / (4 * (energy + 1e-06))

    def put(at_row, at_col, value):
        high, low = split(value)
        rows, cols = slice(at_row * 128, at_row * 128 + 128), slice(at_col * 128, at_col * 128 + 128)
        gram[rows, cols] = high
        gram_low[rows, cols] = low

    for k in range(2):
        for row in range(4):
            here = 4 * k + row
            after, before = (row + 1) % 4, (row + 3) % 4
            side = k if row < 2 else 1 - k
            put(here, here, block(k, row, 0) * square)
            put(here, 4 * (1 - k) + row, block(k, row, 1) * square)
            for one, two, b in (
                (here, 4 * k + after, 2),
                (here, 4 * (1 - k) + after, 3),
                (4 * k + before, 4 * side + after, 4),
            ):
                value = block(k, row, b) * square
                put(one, two, value)
                put(two, one, value.T)

    mine = pl.ds(pl.multiple_of(y * 128, 128), 128)
    column = lax.broadcasted_iota(jnp.int32, (128, NV), 1) - y * 128
    unit = (column == lax.broadcasted_iota(jnp.int32, (128, NV), 0)).astype(F32)
    state[0] = 1.5 * unit - 0.5 * (gram[mine, :].astype(F32) + gram_low[mine, :].astype(F32))

    @pl.loop(0, 12)
    def _(step):
        current = state[0]
        for at, slot in KEEP.items():

            @pl.when(step == at)
            def _():
                state[slot] = current

        slot = jnp.int32(0)
        for at, value in BASE.items():
            slot = jnp.where(step == at, value, slot)
        high, low = split(current)
        twice = mm(jnp.concatenate([high, low], axis=0), gram[...])
        product = (twice[:128] + twice[128:]) + mm(high, gram_low[...])
        state[0] = 1.5 * state[slot] - 0.5 * product

    scale = jnp.sqrt(square) * math.sqrt(total_rows)
    high, low = split(state[0].T * scale)
    factor[:, :128] = high
    factor[:, 128:] = low

    rhs = jnp.concatenate(
        [
            factor[pl.ds(pl.multiple_of((4 * k + lax.rem(y + dy, 4)) * 128, 128), 128), :]
            for k, dy in PIECES
        ],
        axis=0,
    )
    ordered[...] = rhs
    chunk = 256
    half = out_ref.shape[0] // 2
    for part in range(2):

        @pl.loop(0, half // chunk)
        def _(step):
            within = pl.ds(pl.multiple_of(step * chunk, chunk), chunk)
            rows = pl.ds(pl.multiple_of(part * half + step * chunk, chunk), chunk)
            parts = [natural(refs, within, part) for refs in x_refs]
            lhs = jnp.concatenate(split(jnp.concatenate(parts, axis=1)), axis=0)
            out_ref[rows, :] = fold(mm(lhs, ordered[...]))


def finish(total_rows, y, gram_a, gram_b, pieces):
    operands = [chunk for piece in pieces for chunk in piece]
    rows, cols = 2 * operands[0].shape[0], operands[0].shape[1]
    return pl.pallas_call(
        functools.partial(finish_kernel, total_rows),
        out_shape=jax.ShapeDtypeStruct((rows, cols), F32),
        in_specs=[SMEM_SPEC] + [VMEM_SPEC] * (2 + len(operands)),
        out_specs=VMEM_SPEC,
        scratch_shapes=[
            pltpu.VMEM((NV, NV), BF),
            pltpu.VMEM((NV, NV), BF),
            pltpu.VMEM((3, cols, NV), F32),
            pltpu.VMEM((NV, 2 * cols), BF),
            pltpu.VMEM((NV, 2 * cols), BF),
        ],
        compiler_params=pltpu.CompilerParams(vmem_limit_bytes=40 * 2**20),
        cost_estimate=cost(12 * 6 * cols * NV * NV, 4 * rows * cols * 9),
        name="finish",
    )(y, gram_a, gram_b, *operands)


def on_device(vectors, hamiltonian, column_blocks, live_counts, lower_bound, upper_bound):
    rows_dev, panel_cols = vectors.shape
    block_rows, slot_count, block_size, _ = hamiltonian.shape
    row_count, vec_count = lax.axis_size("row"), lax.axis_size("vec")
    first_row = lax.axis_index("row") * block_rows
    local = (column_blocks - first_row + block_rows) % (block_rows * row_count)
    live = jnp.arange(slot_count, dtype=jnp.int32)[None, :] < live_counts[:, None]
    cols = jnp.where(live, jnp.minimum(local, 3 * block_rows - 1), 3 * block_rows).reshape(-1)
    centre = (upper_bound[0] + lower_bound[0]) / 2
    radius = (upper_bound[0] - lower_bound[0]) / 2
    coef = jnp.stack([centre, 1.0 / radius])
    y = (lax.axis_index("vec") // 2)[None].astype(jnp.int32)

    def from_row(value, step):
        return lax.ppermute(value, "row", [((i + step) % row_count, i) for i in range(row_count)])

    def from_y(value, step):
        return lax.ppermute(
            value, "vec", [((i + 2 * step) % vec_count, i) for i in range(vec_count)]
        )

    def swap(value):
        return lax.ppermute(value, "vec", [(i, i ^ 1) for i in range(vec_count)])

    blocks = pack(vectors.reshape(block_rows, block_size, panel_cols))
    split_h = split_blocks(hamiltonian)

    def applied(second, operand, prev=None):
        right = from_row(operand, 1)
        left = from_row(operand, -1)
        return apply_field(second, cols, coef, split_h, left, operand, right, prev)

    own, own_s, up, up_s, down, down_s, across, across_s = ([] for _ in range(8))
    for chunk in range(CHUNKS):
        first = applied(False, blocks[chunk])
        second = applied(True, first, blocks[chunk])
        own.append(second.reshape(rows_dev // 2, panel_cols))
        up.append(from_y(own[-1], 1))
        down.append(from_y(own[-1], -1))
        own_s.append(swap(own[-1]))
        up_s.append(swap(up[-1]))
        down_s.append(swap(down[-1]))
        across.append(from_y((up, down)[chunk][-1], (1, -1)[chunk]))
        across_s.append(swap(across[-1]))
    share = gram_share(y, (own, own_s, up, up_s, down))
    strip = share.shape[0] // row_count
    parts = lax.all_to_all(
        share.reshape(row_count, strip, -1), "row", split_axis=0, concat_axis=0, tiled=True
    )
    part = jnp.sum(parts, axis=0)
    groups = [
        [r * vec_count + v for r in range(row_count) for v in range(core, vec_count, 2)]
        for core in range(2)
    ]
    members = row_count * vec_count // 2
    gram_a = lax.all_to_all(
        jnp.broadcast_to(part[None], (members,) + part.shape),
        ("row", "vec"),
        split_axis=0,
        concat_axis=0,
        tiled=True,
        axis_index_groups=groups,
    ).reshape(row_count, vec_count // 2, strip, -1)
    gram_b = swap(gram_a)
    pieces = (own, own_s, up, up_s, down, down_s, across, across_s)
    return finish(rows_dev * row_count, y, gram_a, gram_b, pieces)


def solution(mesh):
    placed = (P("row", "vec"), P("row", None, None, None), P("row", None), P("row"), P(), P())

    return jax.shard_map(
        on_device, mesh=mesh, in_specs=placed, out_specs=P("row", "vec"), check_vma=False
    )
```

```python
import functools
import math

import jax
import jax.numpy as jnp
from jax import lax
from jax.experimental import pallas as pl
from jax.experimental.pallas import tpu as pltpu
from jax.sharding import PartitionSpec as P


NV = 1024
BF = jnp.bfloat16
F32 = jnp.float32


def split(x):
    high = x.astype(BF)
    return high, (x - high.astype(F32)).astype(BF)


def fold(full):
    rows, cols = full.shape[0] // 2, full.shape[1] // 2
    return (full[:rows, :cols] + full[rows:, :cols]) + (full[:rows, cols:] + full[rows:, cols:])


def mm(a, b):
    return jnp.dot(a, b, preferred_element_type=F32)


def cost(flops, moved):
    return pl.CostEstimate(flops=flops, bytes_accessed=moved, transcendentals=0)


DEPTH = 4


def split_kernel(h_ref, o_ref, buffer, arrived):
    count, size = o_ref.shape[0], h_ref.shape[-1]

    def fetch(row, slot):
        return pltpu.make_async_copy(h_ref.at[row], buffer.at[slot], arrived.at[slot])

    for slot in range(DEPTH):
        fetch(slot, slot).start()

    @pl.loop(0, count)
    def _(row):
        slot = lax.rem(row, DEPTH)
        fetch(row, slot).wait()

        @pl.loop(0, o_ref.shape[1])
        def _(k):
            high, low = split(buffer[slot, k])
            o_ref[row, k, :size, :] = high
            o_ref[row, k, size:, :] = low

        @pl.when(row + DEPTH < count)
        def _():
            fetch(row + DEPTH, slot).start()


def split_blocks(hamiltonian):
    block_rows, slots, size, _ = hamiltonian.shape
    return pl.pallas_call(
        split_kernel,
        out_shape=jax.ShapeDtypeStruct((block_rows, slots, 2 * size, size), BF),
        in_specs=[pl.BlockSpec(memory_space=pl.ANY)],
        out_specs=pl.BlockSpec(memory_space=pltpu.VMEM),
        scratch_shapes=[
            pltpu.VMEM((DEPTH, slots, size, size), F32),
            pltpu.SemaphoreType.DMA((DEPTH,)),
        ],
        compiler_params=pltpu.CompilerParams(vmem_limit_bytes=30 * 2**20),
        cost_estimate=cost(0, 8 * block_rows * slots * size * size),
        name="split_blocks",
    )(hamiltonian)


SMEM_SPEC = pl.BlockSpec(memory_space=pltpu.SMEM)
VMEM_SPEC = pl.BlockSpec(memory_space=pltpu.VMEM)


CHUNKS = 2


def lanes_low(shape):
    return lax.broadcasted_iota(jnp.int32, shape, 1) < shape[1] // 2


def turn(x):
    return pltpu.roll(x, x.shape[1] // 2, 1)


def pack_kernel(v_ref, a_ref, b_ref):
    low = lanes_low(v_ref.shape[1:])
    half = a_ref.shape[0]

    @pl.loop(0, half)
    def _(j):
        one, two = v_ref[j], v_ref[j + half]
        a_ref[j] = jnp.where(low, one, turn(two))
        b_ref[j] = jnp.where(low, turn(one), two)


def pack(blocks):
    count, size, cols = blocks.shape
    shape = jax.ShapeDtypeStruct((count // 2, size, cols), F32)
    return pl.pallas_call(
        pack_kernel,
        out_shape=(shape, shape),
        in_specs=[VMEM_SPEC],
        out_specs=(VMEM_SPEC, VMEM_SPEC),
        compiler_params=pltpu.CompilerParams(vmem_limit_bytes=30 * 2**20),
        cost_estimate=cost(0, 8 * blocks.size),
        name="pack",
    )(blocks)


UNROLL = 4


def field_kernel(second, cols_ref, coef_ref, h_ref, left_ref, own_ref, right_ref, *rest):
    if second:
        prev_ref, o_ref, wide = rest
    else:
        o_ref, wide = rest
    count, slots = h_ref.shape[:2]
    half = count // 2
    low = lanes_low(own_ref.shape[1:])
    for part, ref in enumerate((left_ref, own_ref, right_ref)):

        @pl.loop(0, half, unroll=2)
        def _(j):
            value = ref[j]
            high = value.astype(BF).astype(F32)
            rest_of = value - high
            wide[part * count + j] = jnp.where(low, high, turn(rest_of)).astype(BF)
            wide[part * count + half + j] = jnp.where(low, turn(high), rest_of).astype(BF)

    wide[3 * count] = jnp.zeros(wide.shape[1:], BF)
    centre, inverse = coef_ref[0], coef_ref[1]

    def row(i):
        lhs = jnp.concatenate([h_ref[i, k] for k in range(slots)], axis=1)
        rhs = jnp.concatenate([wide[cols_ref[i * slots + k]] for k in range(slots)], axis=0)
        full = mm(lhs, rhs)
        full = full[: full.shape[0] // 2] + full[full.shape[0] // 2 :]
        return full + turn(full)

    @pl.loop(0, half // UNROLL)
    def _(step):
        for within in range(UNROLL):
            i = step * UNROLL + within
            summed = jnp.where(low, row(i), row(i + half))
            result = (summed - centre * own_ref[i]) * inverse
            if second:
                result = 2.0 * result - prev_ref[i]
            o_ref[i] = result


def apply_field(second, cols, coef, split_h, left, own, right, prev=None):
    block_rows, slots, _, size = split_h.shape
    operands = [split_h, left, own, right] + ([prev] if second else [])
    return pl.pallas_call(
        functools.partial(field_kernel, second),
        out_shape=jax.ShapeDtypeStruct(own.shape, F32),
        in_specs=[SMEM_SPEC] * 2 + [VMEM_SPEC] * len(operands),
        out_specs=VMEM_SPEC,
        scratch_shapes=[pltpu.VMEM((3 * block_rows + 1, size, size), BF)],
        compiler_params=pltpu.CompilerParams(vmem_limit_bytes=30 * 2**20),
        cost_estimate=cost(8 * block_rows * slots * size**3, 2 * split_h.size),
        name="field",
    )(cols, coef, *operands)


def natural(refs, rows, part):
    a, b = (ref[rows, :] for ref in refs)
    low = lanes_low(a.shape)
    return jnp.where(low, turn(a), b) if part else jnp.where(low, a, turn(b))


GRAM_BLOCKS = 5
NEAR_BLOCKS = 2


def gram_product(left, right):
    total = None
    for part in range(2):
        lhs = jnp.concatenate(split(natural(left, slice(None), part).T), axis=0)
        rhs = jnp.concatenate(split(natural(right, slice(None), part)), axis=1)
        term = mm(lhs, rhs)
        total = term if total is None else total + term
    return fold(total)


def columns_of(ref, block):
    return ref.at[:, block * 128 : (block + 1) * 128]


def near_kernel(*rest):
    own, beside = (rest[2 * n : 2 * n + 2] for n in range(2))
    out_ref = rest[4]
    for block, refs in enumerate((own, beside)):
        columns_of(out_ref, block)[...] = gram_product(own, refs)


def far_kernel(y_ref, near_ref, *rest):
    own, up, up_s, down = (rest[2 * n : 2 * n + 2] for n in range(4))
    out_ref = rest[8]
    out_ref[:, : NEAR_BLOCKS * 128] = near_ref[...]
    columns_of(out_ref, 2)[...] = gram_product(own, up)
    columns_of(out_ref, 3)[...] = gram_product(own, up_s)

    @pl.when(y_ref[0] < 2)
    def _():
        columns_of(out_ref, 4)[...] = gram_product(down, up)

    @pl.when(y_ref[0] >= 2)
    def _():
        columns_of(out_ref, 4)[...] = gram_product(down, up_s)


def gram_call(kernel, blocks, products, before, pieces):
    operands = [chunk for piece in pieces for chunk in piece]
    rows, cols = operands[0].shape
    return pl.pallas_call(
        kernel,
        out_shape=jax.ShapeDtypeStruct((cols, blocks * cols), F32),
        in_specs=([SMEM_SPEC, VMEM_SPEC] if before else []) + [VMEM_SPEC] * len(operands),
        out_specs=VMEM_SPEC,
        compiler_params=pltpu.CompilerParams(vmem_limit_bytes=30 * 2**20),
        cost_estimate=cost(16 * rows * cols * cols * products, 4 * rows * cols * len(operands)),
    )(*before, *operands)


KEEP = {0: 1, 3: 2, 4: 1, 8: 1}
BASE = {2: 1, 6: 1, 10: 1, 11: 2}
PIECES = ((0, 0), (1, 0), (0, 1), (1, 1), (0, 3), (1, 3), (0, 2), (1, 2))


def finish_kernel(total_rows, y_ref, ga_ref, gb_ref, *rest):
    x_refs = [rest[2 * n : 2 * n + 2] for n in range(len(PIECES))]
    out_ref, gram, gram_low, state, factor, ordered = rest[2 * len(PIECES) :]
    grams = (ga_ref, gb_ref)
    y = y_ref[0]

    diagonal = lax.broadcasted_iota(jnp.int32, (128, 128), 0) == lax.broadcasted_iota(
        jnp.int32, (128, 128), 1
    )

    def block(k, row, b):
        return grams[k][:, row, :, b * 128 : (b + 1) * 128].reshape(128, 128)

    trace = jnp.zeros((128, 128), F32)
    for k in range(2):
        for row in range(4):
            trace += jnp.where(diagonal, block(k, row, 0), 0.0)
    energy = jnp.sum(jnp.sum(trace, axis=0, keepdims=True), axis=1, keepdims=True)
    square = NV / (4 * (energy + 1e-06))

    def put(at_row, at_col, value):
        high, low = split(value)
        rows, cols = slice(at_row * 128, at_row * 128 + 128), slice(at_col * 128, at_col * 128 + 128)
        gram[rows, cols] = high
        gram_low[rows, cols] = low

    for k in range(2):
        for row in range(4):
            here = 4 * k + row
            after, before = (row + 1) % 4, (row + 3) % 4
            side = k if row < 2 else 1 - k
            put(here, here, block(k, row, 0) * square)
            put(here, 4 * (1 - k) + row, block(k, row, 1) * square)
            for one, two, b in (
                (here, 4 * k + after, 2),
                (here, 4 * (1 - k) + after, 3),
                (4 * k + before, 4 * side + after, 4),
            ):
                value = block(k, row, b) * square
                put(one, two, value)
                put(two, one, value.T)

    mine = pl.ds(pl.multiple_of(y * 128, 128), 128)
    column = lax.broadcasted_iota(jnp.int32, (128, NV), 1) - y * 128
    unit = (column == lax.broadcasted_iota(jnp.int32, (128, NV), 0)).astype(F32)
    state[0] = 1.5 * unit - 0.5 * (gram[mine, :].astype(F32) + gram_low[mine, :].astype(F32))

    @pl.loop(0, 12)
    def _(step):
        current = state[0]
        for at, slot in KEEP.items():

            @pl.when(step == at)
            def _():
                state[slot] = current

        slot = jnp.int32(0)
        for at, value in BASE.items():
            slot = jnp.where(step == at, value, slot)
        high, low = split(current)
        twice = mm(jnp.concatenate([high, low], axis=0), gram[...])
        product = (twice[:128] + twice[128:]) + mm(high, gram_low[...])
        state[0] = 1.5 * state[slot] - 0.5 * product

    scale = jnp.sqrt(square) * math.sqrt(total_rows)
    high, low = split(state[0].T * scale)
    factor[:, :128] = high
    factor[:, 128:] = low

    rhs = jnp.concatenate(
        [
            factor[pl.ds(pl.multiple_of((4 * k + lax.rem(y + dy, 4)) * 128, 128), 128), :]
            for k, dy in PIECES
        ],
        axis=0,
    )
    ordered[...] = rhs
    chunk = 256
    half = out_ref.shape[0] // 2
    for part in range(2):

        @pl.loop(0, half // chunk, unroll=2)
        def _(step):
            within = pl.ds(pl.multiple_of(step * chunk, chunk), chunk)
            rows = pl.ds(pl.multiple_of(part * half + step * chunk, chunk), chunk)
            parts = [natural(refs, within, part) for refs in x_refs]
            lhs = jnp.concatenate(split(jnp.concatenate(parts, axis=1)), axis=0)
            out_ref[rows, :] = fold(mm(lhs, ordered[...]))


def finish(total_rows, y, gram_a, gram_b, pieces):
    operands = [chunk for piece in pieces for chunk in piece]
    rows, cols = 2 * operands[0].shape[0], operands[0].shape[1]
    return pl.pallas_call(
        functools.partial(finish_kernel, total_rows),
        out_shape=jax.ShapeDtypeStruct((rows, cols), F32),
        in_specs=[SMEM_SPEC] + [VMEM_SPEC] * (2 + len(operands)),
        out_specs=VMEM_SPEC,
        scratch_shapes=[
            pltpu.VMEM((NV, NV), BF),
            pltpu.VMEM((NV, NV), BF),
            pltpu.VMEM((3, cols, NV), F32),
            pltpu.VMEM((NV, 2 * cols), BF),
            pltpu.VMEM((NV, 2 * cols), BF),
        ],
        compiler_params=pltpu.CompilerParams(vmem_limit_bytes=40 * 2**20),
        cost_estimate=cost(12 * 6 * cols * NV * NV, 4 * rows * cols * 9),
        name="finish",
    )(y, gram_a, gram_b, *operands)


def on_device(vectors, hamiltonian, column_blocks, live_counts, lower_bound, upper_bound):
    rows_dev, panel_cols = vectors.shape
    block_rows, slot_count, block_size, _ = hamiltonian.shape
    row_count, vec_count = lax.axis_size("row"), lax.axis_size("vec")
    first_row = lax.axis_index("row") * block_rows
    local = (column_blocks - first_row + block_rows) % (block_rows * row_count)
    live = jnp.arange(slot_count, dtype=jnp.int32)[None, :] < live_counts[:, None]
    cols = jnp.where(live, jnp.minimum(local, 3 * block_rows - 1), 3 * block_rows).reshape(-1)
    centre = (upper_bound[0] + lower_bound[0]) / 2
    radius = (upper_bound[0] - lower_bound[0]) / 2
    coef = jnp.stack([centre, 1.0 / radius])
    y = (lax.axis_index("vec") // 2)[None].astype(jnp.int32)

    def from_row(value, step):
        return lax.ppermute(value, "row", [((i + step) % row_count, i) for i in range(row_count)])

    def from_y(value, step):
        return lax.ppermute(
            value, "vec", [((i + 2 * step) % vec_count, i) for i in range(vec_count)]
        )

    def swap(value):
        return lax.ppermute(value, "vec", [(i, i ^ 1) for i in range(vec_count)])

    blocks = pack(vectors.reshape(block_rows, block_size, panel_cols))
    split_h = split_blocks(hamiltonian)

    def applied(second, operand, prev=None):
        right = from_row(operand, 1)
        left = from_row(operand, -1)
        return apply_field(second, cols, coef, split_h, left, operand, right, prev)

    own, own_s, up, up_s, down, down_s, across, across_s = ([] for _ in range(8))
    for chunk in range(CHUNKS):
        first = applied(False, blocks[chunk])
        second = applied(True, first, blocks[chunk])
        own.append(second.reshape(rows_dev // 2, panel_cols))
        up.append(from_y(own[-1], 1))
        down.append(from_y(own[-1], -1))
        own_s.append(swap(own[-1]))
        up_s.append(swap(up[-1]))
        down_s.append(swap(down[-1]))
        across.append(from_y((up, down)[chunk][-1], (1, -1)[chunk]))
        across_s.append(swap(across[-1]))
    near = gram_call(near_kernel, NEAR_BLOCKS, 2, (), (own, own_s))
    share = gram_call(far_kernel, GRAM_BLOCKS, 3, (y, near), (own, up, up_s, down))
    strip = share.shape[0] // row_count
    parts = lax.all_to_all(
        share.reshape(row_count, strip, -1), "row", split_axis=0, concat_axis=0, tiled=True
    )
    part = jnp.sum(parts, axis=0)
    groups = [
        [r * vec_count + v for r in range(row_count) for v in range(core, vec_count, 2)]
        for core in range(2)
    ]
    members = row_count * vec_count // 2
    gram_a = lax.all_to_all(
        jnp.broadcast_to(part[None], (members,) + part.shape),
        ("row", "vec"),
        split_axis=0,
        concat_axis=0,
        tiled=True,
        axis_index_groups=groups,
    ).reshape(row_count, vec_count // 2, strip, -1)
    gram_b = swap(gram_a)
    pieces = (own, own_s, up, up_s, down, down_s, across, across_s)
    return finish(rows_dev * row_count, y, gram_a, gram_b, pieces)


def solution(mesh):
    placed = (P("row", "vec"), P("row", None, None, None), P("row", None), P("row"), P(), P())

    return jax.shard_map(
        on_device, mesh=mesh, in_specs=placed, out_specs=P("row", "vec"), check_vma=False
    )
```

```python
import functools
import math

import jax
import jax.numpy as jnp
from jax import lax
from jax.experimental import pallas as pl
from jax.experimental.pallas import tpu as pltpu
from jax.sharding import PartitionSpec as P


NV = 1024
BF = jnp.bfloat16
F32 = jnp.float32


def split(x):
    high = x.astype(BF)
    return high, (x - high.astype(F32)).astype(BF)


def fold(full):
    rows, cols = full.shape[0] // 2, full.shape[1] // 2
    return (full[:rows, :cols] + full[rows:, :cols]) + (full[:rows, cols:] + full[rows:, cols:])


def mm(a, b):
    return jnp.dot(a, b, preferred_element_type=F32)


def cost(flops, moved):
    return pl.CostEstimate(flops=flops, bytes_accessed=moved, transcendentals=0)


DEPTH = 4


def split_kernel(h_ref, o_ref, buffer, arrived):
    count, size = o_ref.shape[0], h_ref.shape[-1]

    def fetch(row, slot):
        return pltpu.make_async_copy(h_ref.at[row], buffer.at[slot], arrived.at[slot])

    for slot in range(DEPTH):
        fetch(slot, slot).start()

    @pl.loop(0, count)
    def _(row):
        slot = lax.rem(row, DEPTH)
        fetch(row, slot).wait()

        @pl.loop(0, o_ref.shape[1])
        def _(k):
            high, low = split(buffer[slot, k])
            o_ref[row, k, :size, :] = high
            o_ref[row, k, size:, :] = low

        @pl.when(row + DEPTH < count)
        def _():
            fetch(row + DEPTH, slot).start()


def split_blocks(hamiltonian):
    block_rows, slots, size, _ = hamiltonian.shape
    return pl.pallas_call(
        split_kernel,
        out_shape=jax.ShapeDtypeStruct((block_rows, slots, 2 * size, size), BF),
        in_specs=[pl.BlockSpec(memory_space=pl.ANY)],
        out_specs=pl.BlockSpec(memory_space=pltpu.VMEM),
        scratch_shapes=[
            pltpu.VMEM((DEPTH, slots, size, size), F32),
            pltpu.SemaphoreType.DMA((DEPTH,)),
        ],
        compiler_params=pltpu.CompilerParams(vmem_limit_bytes=30 * 2**20),
        cost_estimate=cost(0, 8 * block_rows * slots * size * size),
        name="split_blocks",
    )(hamiltonian)


SMEM_SPEC = pl.BlockSpec(memory_space=pltpu.SMEM)
VMEM_SPEC = pl.BlockSpec(memory_space=pltpu.VMEM)


CHUNKS = 2


def lanes_low(shape):
    return lax.broadcasted_iota(jnp.int32, shape, 1) < shape[1] // 2


def turn(x):
    return pltpu.roll(x, x.shape[1] // 2, 1)


PACK_GROUPS = 4


def pack_kernel(v_ref, a_ref, b_ref, buffer, arrived):
    low = lanes_low(buffer.shape[1:])
    half = a_ref.shape[0]
    group = half // PACK_GROUPS
    copies = []
    for g in range(PACK_GROUPS):
        for side in range(2):
            blocks = pl.ds(side * half + g * group, group)
            copy = pltpu.make_async_copy(
                v_ref.at[blocks], buffer.at[blocks], arrived.at[2 * g + side]
            )
            copy.start()
            copies.append(copy)
    for g in range(PACK_GROUPS):
        copies[2 * g].wait()
        copies[2 * g + 1].wait()
        for j in range(g * group, (g + 1) * group):
            one, two = buffer[j], buffer[j + half]
            a_ref[j] = jnp.where(low, one, turn(two))
            b_ref[j] = jnp.where(low, turn(one), two)


def pack(blocks):
    count, size, cols = blocks.shape
    shape = jax.ShapeDtypeStruct((count // 2, size, cols), F32)
    return pl.pallas_call(
        pack_kernel,
        out_shape=(shape, shape),
        in_specs=[pl.BlockSpec(memory_space=pl.ANY)],
        out_specs=(VMEM_SPEC, VMEM_SPEC),
        scratch_shapes=[
            pltpu.VMEM(blocks.shape, F32),
            pltpu.SemaphoreType.DMA((2 * PACK_GROUPS,)),
        ],
        compiler_params=pltpu.CompilerParams(vmem_limit_bytes=30 * 2**20),
        cost_estimate=cost(0, 8 * blocks.size),
        name="pack",
    )(blocks)


UNROLL = 4


def field_kernel(second, cols_ref, coef_ref, h_ref, left_ref, own_ref, right_ref, *rest):
    if second:
        prev_ref, o_ref, wide = rest
    else:
        o_ref, wide = rest
    count, slots = h_ref.shape[:2]
    half = count // 2
    low = lanes_low(own_ref.shape[1:])
    for part, ref in enumerate((left_ref, own_ref, right_ref)):

        @pl.loop(0, half, unroll=2)
        def _(j):
            value = ref[j]
            high = value.astype(BF).astype(F32)
            rest_of = value - high
            wide[part * count + j] = jnp.where(low, high, turn(rest_of)).astype(BF)
            wide[part * count + half + j] = jnp.where(low, turn(high), rest_of).astype(BF)

    wide[3 * count] = jnp.zeros(wide.shape[1:], BF)
    centre, inverse = coef_ref[0], coef_ref[1]

    def row(i):
        lhs = jnp.concatenate([h_ref[i, k] for k in range(slots)], axis=1)
        rhs = jnp.concatenate([wide[cols_ref[i * slots + k]] for k in range(slots)], axis=0)
        full = mm(lhs, rhs)
        full = full[: full.shape[0] // 2] + full[full.shape[0] // 2 :]
        return full + turn(full)

    @pl.loop(0, half // UNROLL)
    def _(step):
        for within in range(UNROLL):
            i = step * UNROLL + within
            summed = jnp.where(low, row(i), row(i + half))
            result = (summed - centre * own_ref[i]) * inverse
            if second:
                result = 2.0 * result - prev_ref[i]
            o_ref[i] = result


def apply_field(second, cols, coef, split_h, left, own, right, prev=None):
    block_rows, slots, _, size = split_h.shape
    operands = [split_h, left, own, right] + ([prev] if second else [])
    return pl.pallas_call(
        functools.partial(field_kernel, second),
        out_shape=jax.ShapeDtypeStruct(own.shape, F32),
        in_specs=[SMEM_SPEC] * 2 + [VMEM_SPEC] * len(operands),
        out_specs=VMEM_SPEC,
        scratch_shapes=[pltpu.VMEM((3 * block_rows + 1, size, size), BF)],
        compiler_params=pltpu.CompilerParams(vmem_limit_bytes=30 * 2**20),
        cost_estimate=cost(8 * block_rows * slots * size**3, 2 * split_h.size),
        name="field",
    )(cols, coef, *operands)


def natural(refs, rows, part):
    a, b = (ref[rows, :] for ref in refs)
    low = lanes_low(a.shape)
    return jnp.where(low, turn(a), b) if part else jnp.where(low, a, turn(b))


GRAM_BLOCKS = 5
NEAR_BLOCKS = 2


def turned(refs, part):
    half = refs[0].shape[1] // 2
    lines = slice(part * half, (part + 1) * half)
    both = jnp.concatenate([ref[...].T[lines] for ref in refs], axis=0)
    return jnp.concatenate(split(both), axis=0)


def paired(refs, part):
    return jnp.concatenate(split(natural(refs, slice(None), part)), axis=1)


def columns_of(ref, block):
    return ref.at[:, block * 128 : (block + 1) * 128]


def near_kernel(*rest):
    own, beside = (rest[2 * n : 2 * n + 2] for n in range(2))
    out_ref, lhs = rest[4:]
    for part in range(2):
        lhs[part] = turned(own, part)
    for block, refs in enumerate((own, beside)):
        terms = [mm(lhs[part], paired(refs, part)) for part in range(2)]
        columns_of(out_ref, block)[...] = fold(terms[0] + terms[1])


def far_kernel(y_ref, near_ref, lhs_ref, *rest):
    up, up_s, down = (rest[2 * n : 2 * n + 2] for n in range(3))
    out_ref, rhs = rest[6:]
    out_ref[:, : NEAR_BLOCKS * 128] = near_ref[...]
    for which, refs in enumerate((up, up_s)):
        for part in range(2):
            rhs[2 * which + part] = paired(refs, part)
        terms = [mm(lhs_ref[part], rhs[2 * which + part]) for part in range(2)]
        columns_of(out_ref, NEAR_BLOCKS + which)[...] = fold(terms[0] + terms[1])
    side = jnp.where(y_ref[0] < 2, 0, 2)
    terms = [mm(turned(down, part), rhs[side + part]) for part in range(2)]
    columns_of(out_ref, 4)[...] = fold(terms[0] + terms[1])


def flat(pieces):
    return [chunk for piece in pieces for chunk in piece]


def gram_near(pieces):
    operands = flat(pieces)
    rows, cols = operands[0].shape
    return pl.pallas_call(
        near_kernel,
        out_shape=(
            jax.ShapeDtypeStruct((cols, NEAR_BLOCKS * cols), F32),
            jax.ShapeDtypeStruct((2, 2 * cols, rows), BF),
        ),
        in_specs=[VMEM_SPEC] * len(operands),
        out_specs=(VMEM_SPEC, VMEM_SPEC),
        compiler_params=pltpu.CompilerParams(vmem_limit_bytes=30 * 2**20),
        cost_estimate=cost(32 * rows * cols * cols, 16 * rows * cols),
        name="gram_near",
    )(*operands)


def gram_far(y, near, lhs, pieces):
    operands = flat(pieces)
    rows, cols = operands[0].shape
    return pl.pallas_call(
        far_kernel,
        out_shape=jax.ShapeDtypeStruct((cols, GRAM_BLOCKS * cols), F32),
        in_specs=[SMEM_SPEC] + [VMEM_SPEC] * (2 + len(operands)),
        out_specs=VMEM_SPEC,
        scratch_shapes=[pltpu.VMEM((4, rows, 2 * cols), BF)],
        compiler_params=pltpu.CompilerParams(vmem_limit_bytes=30 * 2**20),
        cost_estimate=cost(48 * rows * cols * cols, 24 * rows * cols),
        name="gram_far",
    )(y, near, lhs, *operands)


KEEP = {0: 1, 3: 2, 4: 1, 8: 1}
BASE = {2: 1, 6: 1, 10: 1, 11: 2}
PIECES = ((0, 0), (1, 0), (0, 1), (1, 1), (0, 3), (1, 3), (0, 2), (1, 2))


def finish_kernel(total_rows, y_ref, ga_ref, gb_ref, *rest):
    x_refs = [rest[2 * n : 2 * n + 2] for n in range(len(PIECES))]
    out_ref, gram, gram_low, state, factor, ordered = rest[2 * len(PIECES) :]
    grams = (ga_ref, gb_ref)
    y = y_ref[0]

    diagonal = lax.broadcasted_iota(jnp.int32, (128, 128), 0) == lax.broadcasted_iota(
        jnp.int32, (128, 128), 1
    )

    def block(k, row, b):
        return grams[k][:, row, :, b * 128 : (b + 1) * 128].reshape(128, 128)

    trace = jnp.zeros((128, 128), F32)
    for k in range(2):
        for row in range(4):
            trace += jnp.where(diagonal, block(k, row, 0), 0.0)
    energy = jnp.sum(jnp.sum(trace, axis=0, keepdims=True), axis=1, keepdims=True)
    square = NV / (4 * (energy + 1e-06))

    def put(at_row, at_col, value):
        high, low = split(value)
        rows, cols = slice(at_row * 128, at_row * 128 + 128), slice(at_col * 128, at_col * 128 + 128)
        gram[rows, cols] = high
        gram_low[rows, cols] = low

    for k in range(2):
        for row in range(4):
            here = 4 * k + row
            after, before = (row + 1) % 4, (row + 3) % 4
            side = k if row < 2 else 1 - k
            put(here, here, block(k, row, 0) * square)
            put(here, 4 * (1 - k) + row, block(k, row, 1) * square)
            for one, two, b in (
                (here, 4 * k + after, 2),
                (here, 4 * (1 - k) + after, 3),
                (4 * k + before, 4 * side + after, 4),
            ):
                value = block(k, row, b) * square
                put(one, two, value)
                put(two, one, value.T)

    mine = pl.ds(pl.multiple_of(y * 128, 128), 128)
    column = lax.broadcasted_iota(jnp.int32, (128, NV), 1) - y * 128
    unit = (column == lax.broadcasted_iota(jnp.int32, (128, NV), 0)).astype(F32)
    state[0] = 1.5 * unit - 0.5 * (gram[mine, :].astype(F32) + gram_low[mine, :].astype(F32))

    @pl.loop(0, 12)
    def _(step):
        current = state[0]
        for at, slot in KEEP.items():

            @pl.when(step == at)
            def _():
                state[slot] = current

        slot = jnp.int32(0)
        for at, value in BASE.items():
            slot = jnp.where(step == at, value, slot)
        high, low = split(current)
        twice = mm(jnp.concatenate([high, low], axis=0), gram[...])
        product = (twice[:128] + twice[128:]) + mm(high, gram_low[...])
        state[0] = 1.5 * state[slot] - 0.5 * product

    scale = jnp.sqrt(square) * math.sqrt(total_rows)
    high, low = split(state[0].T * scale)
    factor[:, :128] = high
    factor[:, 128:] = low

    rhs = jnp.concatenate(
        [
            factor[pl.ds(pl.multiple_of((4 * k + lax.rem(y + dy, 4)) * 128, 128), 128), :]
            for k, dy in PIECES
        ],
        axis=0,
    )
    ordered[...] = rhs
    chunk = 256
    half = out_ref.shape[0] // 2
    for part in range(2):

        @pl.loop(0, half // chunk, unroll=2)
        def _(step):
            within = pl.ds(pl.multiple_of(step * chunk, chunk), chunk)
            rows = pl.ds(pl.multiple_of(part * half + step * chunk, chunk), chunk)
            parts = [natural(refs, within, part) for refs in x_refs]
            high, low = split(jnp.concatenate(parts, axis=1))
            full = mm(high, ordered[...])
            cols = full.shape[1] // 2
            out_ref[rows, :] = (full[:, :cols] + full[:, cols:]) + mm(low, ordered[:, :cols])


def finish(total_rows, y, gram_a, gram_b, pieces):
    operands = [chunk for piece in pieces for chunk in piece]
    rows, cols = 2 * operands[0].shape[0], operands[0].shape[1]
    return pl.pallas_call(
        functools.partial(finish_kernel, total_rows),
        out_shape=jax.ShapeDtypeStruct((rows, cols), F32),
        in_specs=[SMEM_SPEC] + [VMEM_SPEC] * (2 + len(operands)),
        out_specs=VMEM_SPEC,
        scratch_shapes=[
            pltpu.VMEM((NV, NV), BF),
            pltpu.VMEM((NV, NV), BF),
            pltpu.VMEM((3, cols, NV), F32),
            pltpu.VMEM((NV, 2 * cols), BF),
            pltpu.VMEM((NV, 2 * cols), BF),
        ],
        compiler_params=pltpu.CompilerParams(vmem_limit_bytes=40 * 2**20),
        cost_estimate=cost(12 * 6 * cols * NV * NV, 4 * rows * cols * 9),
        name="finish",
    )(y, gram_a, gram_b, *operands)


def on_device(vectors, hamiltonian, column_blocks, live_counts, lower_bound, upper_bound):
    rows_dev, panel_cols = vectors.shape
    block_rows, slot_count, block_size, _ = hamiltonian.shape
    row_count, vec_count = lax.axis_size("row"), lax.axis_size("vec")
    first_row = lax.axis_index("row") * block_rows
    local = (column_blocks - first_row + block_rows) % (block_rows * row_count)
    live = jnp.arange(slot_count, dtype=jnp.int32)[None, :] < live_counts[:, None]
    cols = jnp.where(live, jnp.minimum(local, 3 * block_rows - 1), 3 * block_rows).reshape(-1)
    centre = (upper_bound[0] + lower_bound[0]) / 2
    radius = (upper_bound[0] - lower_bound[0]) / 2
    coef = jnp.stack([centre, 1.0 / radius])
    y = (lax.axis_index("vec") // 2)[None].astype(jnp.int32)

    def from_row(value, step):
        return lax.ppermute(value, "row", [((i + step) % row_count, i) for i in range(row_count)])

    def from_y(value, step):
        return lax.ppermute(
            value, "vec", [((i + 2 * step) % vec_count, i) for i in range(vec_count)]
        )

    def swap(value):
        return lax.ppermute(value, "vec", [(i, i ^ 1) for i in range(vec_count)])

    blocks = pack(vectors.reshape(block_rows, block_size, panel_cols))
    split_h = split_blocks(hamiltonian)

    def applied(second, operand, prev=None):
        right = from_row(operand, 1)
        left = from_row(operand, -1)
        return apply_field(second, cols, coef, split_h, left, operand, right, prev)

    own, own_s, up, up_s, down, down_s, across, across_s = ([] for _ in range(8))
    for chunk in range(CHUNKS):
        first = applied(False, blocks[chunk])
        second = applied(True, first, blocks[chunk])
        own.append(second.reshape(rows_dev // 2, panel_cols))
        up.append(from_y(own[-1], 1))
        down.append(from_y(own[-1], -1))
        own_s.append(swap(own[-1]))
        up_s.append(swap(up[-1]))
        down_s.append(swap(down[-1]))
        across.append(from_y((up, down)[chunk][-1], (1, -1)[chunk]))
        across_s.append(swap(across[-1]))
    near, lhs = gram_near((own, own_s))
    share = gram_far(y, near, lhs, (up, up_s, down))
    strip = share.shape[0] // row_count
    parts = lax.all_to_all(
        share.reshape(row_count, strip, -1), "row", split_axis=0, concat_axis=0, tiled=True
    )
    part = jnp.sum(parts, axis=0)
    groups = [
        [r * vec_count + v for r in range(row_count) for v in range(core, vec_count, 2)]
        for core in range(2)
    ]
    members = row_count * vec_count // 2
    gram_a = lax.all_to_all(
        jnp.broadcast_to(part[None], (members,) + part.shape),
        ("row", "vec"),
        split_axis=0,
        concat_axis=0,
        tiled=True,
        axis_index_groups=groups,
    ).reshape(row_count, vec_count // 2, strip, -1)
    gram_b = swap(gram_a)
    pieces = (own, own_s, up, up_s, down, down_s, across, across_s)
    return finish(rows_dev * row_count, y, gram_a, gram_b, pieces)


def solution(mesh):
    placed = (P("row", "vec"), P("row", None, None, None), P("row", None), P("row"), P(), P())

    return jax.shard_map(
        on_device, mesh=mesh, in_specs=placed, out_specs=P("row", "vec"), check_vma=False
    )
```

```python
import functools
import math

import jax
import jax.numpy as jnp
from jax import lax
from jax.experimental import pallas as pl
from jax.experimental.pallas import tpu as pltpu
from jax.sharding import PartitionSpec as P


NV = 1024
BF = jnp.bfloat16
F32 = jnp.float32


def split(x):
    high = x.astype(BF)
    return high, (x - high.astype(F32)).astype(BF)


def fold(full):
    rows, cols = full.shape[0] // 2, full.shape[1] // 2
    return (full[:rows, :cols] + full[rows:, :cols]) + (full[:rows, cols:] + full[rows:, cols:])


def mm(a, b):
    return jnp.dot(a, b, preferred_element_type=F32)


def cost(flops, moved):
    return pl.CostEstimate(flops=flops, bytes_accessed=moved, transcendentals=0)


DEPTH = 4


def split_kernel(h_ref, o_ref, buffer, arrived):
    count, size = o_ref.shape[0], h_ref.shape[-1]

    def fetch(row, slot):
        return pltpu.make_async_copy(h_ref.at[row], buffer.at[slot], arrived.at[slot])

    for slot in range(DEPTH):
        fetch(slot, slot).start()

    @pl.loop(0, count)
    def _(row):
        slot = lax.rem(row, DEPTH)
        fetch(row, slot).wait()

        @pl.loop(0, o_ref.shape[1])
        def _(k):
            high, low = split(buffer[slot, k])
            o_ref[row, k, :size, :] = high
            o_ref[row, k, size:, :] = low

        @pl.when(row + DEPTH < count)
        def _():
            fetch(row + DEPTH, slot).start()


def split_blocks(hamiltonian):
    block_rows, slots, size, _ = hamiltonian.shape
    return pl.pallas_call(
        split_kernel,
        out_shape=jax.ShapeDtypeStruct((block_rows, slots, 2 * size, size), BF),
        in_specs=[pl.BlockSpec(memory_space=pl.ANY)],
        out_specs=pl.BlockSpec(memory_space=pltpu.VMEM),
        scratch_shapes=[
            pltpu.VMEM((DEPTH, slots, size, size), F32),
            pltpu.SemaphoreType.DMA((DEPTH,)),
        ],
        compiler_params=pltpu.CompilerParams(vmem_limit_bytes=30 * 2**20),
        cost_estimate=cost(0, 8 * block_rows * slots * size * size),
        name="split_blocks",
    )(hamiltonian)


SMEM_SPEC = pl.BlockSpec(memory_space=pltpu.SMEM)
VMEM_SPEC = pl.BlockSpec(memory_space=pltpu.VMEM)


CHUNKS = 2


def lanes_low(shape):
    return lax.broadcasted_iota(jnp.int32, shape, 1) < shape[1] // 2


def turn(x):
    return pltpu.roll(x, x.shape[1] // 2, 1)


def pack_kernel(v_ref, a_ref, b_ref):
    low = lanes_low(v_ref.shape[1:])
    half = a_ref.shape[0]

    @pl.loop(0, half, unroll=2)
    def _(j):
        one, two = v_ref[j], v_ref[j + half]
        a_ref[j] = jnp.where(low, one, turn(two))
        b_ref[j] = jnp.where(low, turn(one), two)


def pack(blocks):
    count, size, cols = blocks.shape
    shape = jax.ShapeDtypeStruct((count // 2, size, cols), F32)
    return pl.pallas_call(
        pack_kernel,
        out_shape=(shape, shape),
        in_specs=[VMEM_SPEC],
        out_specs=(VMEM_SPEC, VMEM_SPEC),
        compiler_params=pltpu.CompilerParams(vmem_limit_bytes=30 * 2**20),
        cost_estimate=cost(0, 8 * blocks.size),
        name="pack",
    )(blocks)


UNROLL = 4


def field_kernel(second, cols_ref, coef_ref, h_ref, left_ref, own_ref, right_ref, *rest):
    if second:
        prev_ref, o_ref, wide = rest
    else:
        o_ref, wide = rest
    count, slots = h_ref.shape[:2]
    half = count // 2
    low = lanes_low(own_ref.shape[1:])
    for part, ref in enumerate((left_ref, own_ref, right_ref)):

        @pl.loop(0, half, unroll=2)
        def _(j):
            value = ref[j]
            high = value.astype(BF).astype(F32)
            rest_of = value - high
            wide[part * count + j] = jnp.where(low, high, turn(rest_of)).astype(BF)
            wide[part * count + half + j] = jnp.where(low, turn(high), rest_of).astype(BF)

    wide[3 * count] = jnp.zeros(wide.shape[1:], BF)
    centre, inverse = coef_ref[0], coef_ref[1]

    def row(i):
        lhs = jnp.concatenate([h_ref[i, k] for k in range(slots)], axis=1)
        rhs = jnp.concatenate([wide[cols_ref[i * slots + k]] for k in range(slots)], axis=0)
        full = mm(lhs, rhs)
        full = full[: full.shape[0] // 2] + full[full.shape[0] // 2 :]
        return full + turn(full)

    @pl.loop(0, half // UNROLL)
    def _(step):
        for within in range(UNROLL):
            i = step * UNROLL + within
            summed = jnp.where(low, row(i), row(i + half))
            result = (summed - centre * own_ref[i]) * inverse
            if second:
                result = 2.0 * result - prev_ref[i]
            o_ref[i] = result


def apply_field(second, cols, coef, split_h, left, own, right, prev=None):
    block_rows, slots, _, size = split_h.shape
    operands = [split_h, left, own, right] + ([prev] if second else [])
    return pl.pallas_call(
        functools.partial(field_kernel, second),
        out_shape=jax.ShapeDtypeStruct(own.shape, F32),
        in_specs=[SMEM_SPEC] * 2 + [VMEM_SPEC] * len(operands),
        out_specs=VMEM_SPEC,
        scratch_shapes=[pltpu.VMEM((3 * block_rows + 1, size, size), BF)],
        compiler_params=pltpu.CompilerParams(vmem_limit_bytes=30 * 2**20),
        cost_estimate=cost(8 * block_rows * slots * size**3, 2 * split_h.size),
        name="field",
    )(cols, coef, *operands)


def natural(refs, rows, part):
    a, b = (ref[rows, :] for ref in refs)
    low = lanes_low(a.shape)
    return jnp.where(low, turn(a), b) if part else jnp.where(low, a, turn(b))


GRAM_BLOCKS = 5
NEAR_BLOCKS = 2


def turned(refs, part):
    half = refs[0].shape[1] // 2
    lines = slice(part * half, (part + 1) * half)
    both = jnp.concatenate([ref[...].T[lines] for ref in refs], axis=0)
    return jnp.concatenate(split(both), axis=0)


def paired(refs, part):
    return jnp.concatenate(split(natural(refs, slice(None), part)), axis=1)


def columns_of(ref, block):
    return ref.at[:, block * 128 : (block + 1) * 128]


def near_kernel(*rest):
    own, beside = (rest[2 * n : 2 * n + 2] for n in range(2))
    out_ref, lhs = rest[4:]
    for part in range(2):
        lhs[part] = turned(own, part)
    for block, refs in enumerate((own, beside)):
        terms = [mm(lhs[part], paired(refs, part)) for part in range(2)]
        columns_of(out_ref, block)[...] = fold(terms[0] + terms[1])


def fetched(sources, held, arrived):
    copies = [
        pltpu.make_async_copy(ref, held.at[n], arrived.at[n]) for n, ref in enumerate(sources)
    ]
    for copy in copies:
        copy.start()
    return copies, [held.at[n] for n in range(len(sources))]


def far_kernel(y_ref, near_ref, lhs_ref, *rest):
    out_ref, rhs, held, arrived = rest[6:]
    copies, refs = fetched(rest[:6], held, arrived)
    up, up_s, down = (refs[2 * n : 2 * n + 2] for n in range(3))
    out_ref[:, : NEAR_BLOCKS * 128] = near_ref[...]
    for which, refs in enumerate((up, up_s)):
        for copy in copies[2 * which : 2 * which + 2]:
            copy.wait()
        for part in range(2):
            rhs[2 * which + part] = paired(refs, part)
        terms = [mm(lhs_ref[part], rhs[2 * which + part]) for part in range(2)]
        columns_of(out_ref, NEAR_BLOCKS + which)[...] = fold(terms[0] + terms[1])
    for copy in copies[4:]:
        copy.wait()
    side = jnp.where(y_ref[0] < 2, 0, 2)
    terms = [mm(turned(down, part), rhs[side + part]) for part in range(2)]
    columns_of(out_ref, 4)[...] = fold(terms[0] + terms[1])


def flat(pieces):
    return [chunk for piece in pieces for chunk in piece]


def gram_near(pieces):
    operands = flat(pieces)
    rows, cols = operands[0].shape
    return pl.pallas_call(
        near_kernel,
        out_shape=(
            jax.ShapeDtypeStruct((cols, NEAR_BLOCKS * cols), F32),
            jax.ShapeDtypeStruct((2, 2 * cols, rows), BF),
        ),
        in_specs=[VMEM_SPEC] * len(operands),
        out_specs=(VMEM_SPEC, VMEM_SPEC),
        compiler_params=pltpu.CompilerParams(vmem_limit_bytes=30 * 2**20),
        cost_estimate=cost(32 * rows * cols * cols, 16 * rows * cols),
        name="gram_near",
    )(*operands)


def gram_far(y, near, lhs, pieces):
    operands = flat(pieces)
    rows, cols = operands[0].shape
    return pl.pallas_call(
        far_kernel,
        out_shape=jax.ShapeDtypeStruct((cols, GRAM_BLOCKS * cols), F32),
        in_specs=[SMEM_SPEC, VMEM_SPEC, VMEM_SPEC]
        + [pl.BlockSpec(memory_space=pl.ANY)] * len(operands),
        out_specs=VMEM_SPEC,
        scratch_shapes=[
            pltpu.VMEM((4, rows, 2 * cols), BF),
            pltpu.VMEM((len(operands), rows, cols), F32),
            pltpu.SemaphoreType.DMA((len(operands),)),
        ],
        compiler_params=pltpu.CompilerParams(vmem_limit_bytes=30 * 2**20),
        cost_estimate=cost(48 * rows * cols * cols, 24 * rows * cols),
        name="gram_far",
    )(y, near, lhs, *operands)


KEEP = {0: 1, 3: 2, 4: 1, 8: 1}
BASE = {2: 1, 6: 1, 10: 1, 11: 2}
PIECES = ((0, 0), (1, 0), (0, 1), (1, 1), (0, 3), (1, 3), (0, 2), (1, 2))


def finish_kernel(total_rows, y_ref, ga_ref, gb_ref, *rest):
    sources = rest[: 2 * len(PIECES)]
    out_ref, gram, gram_low, state, factor, ordered, held, arrived = rest[2 * len(PIECES) :]
    copies, held_refs = fetched(sources, held, arrived)
    x_refs = [held_refs[2 * n : 2 * n + 2] for n in range(len(PIECES))]
    grams = (ga_ref, gb_ref)
    y = y_ref[0]

    diagonal = lax.broadcasted_iota(jnp.int32, (128, 128), 0) == lax.broadcasted_iota(
        jnp.int32, (128, 128), 1
    )

    def block(k, row, b):
        return grams[k][:, row, :, b * 128 : (b + 1) * 128].reshape(128, 128)

    trace = jnp.zeros((128, 128), F32)
    for k in range(2):
        for row in range(4):
            trace += jnp.where(diagonal, block(k, row, 0), 0.0)
    energy = jnp.sum(jnp.sum(trace, axis=0, keepdims=True), axis=1, keepdims=True)
    square = NV / (4 * (energy + 1e-06))

    def put(at_row, at_col, value):
        high, low = split(value)
        rows, cols = slice(at_row * 128, at_row * 128 + 128), slice(at_col * 128, at_col * 128 + 128)
        gram[rows, cols] = high
        gram_low[rows, cols] = low

    for k in range(2):
        for row in range(4):
            here = 4 * k + row
            after, before = (row + 1) % 4, (row + 3) % 4
            side = k if row < 2 else 1 - k
            put(here, here, block(k, row, 0) * square)
            put(here, 4 * (1 - k) + row, block(k, row, 1) * square)
            for one, two, b in (
                (here, 4 * k + after, 2),
                (here, 4 * (1 - k) + after, 3),
                (4 * k + before, 4 * side + after, 4),
            ):
                value = block(k, row, b) * square
                put(one, two, value)
                put(two, one, value.T)

    mine = pl.ds(pl.multiple_of(y * 128, 128), 128)
    column = lax.broadcasted_iota(jnp.int32, (128, NV), 1) - y * 128
    unit = (column == lax.broadcasted_iota(jnp.int32, (128, NV), 0)).astype(F32)
    state[0] = 1.5 * unit - 0.5 * (gram[mine, :].astype(F32) + gram_low[mine, :].astype(F32))

    @pl.loop(0, 12)
    def _(step):
        current = state[0]
        for at, slot in KEEP.items():

            @pl.when(step == at)
            def _():
                state[slot] = current

        slot = jnp.int32(0)
        for at, value in BASE.items():
            slot = jnp.where(step == at, value, slot)
        high, low = split(current)
        twice = mm(jnp.concatenate([high, low], axis=0), gram[...])
        product = (twice[:128] + twice[128:]) + mm(high, gram_low[...])
        state[0] = 1.5 * state[slot] - 0.5 * product

    scale = jnp.sqrt(square) * math.sqrt(total_rows)
    high, low = split(state[0].T * scale)
    factor[:, :128] = high
    factor[:, 128:] = low

    rhs = jnp.concatenate(
        [
            factor[pl.ds(pl.multiple_of((4 * k + lax.rem(y + dy, 4)) * 128, 128), 128), :]
            for k, dy in PIECES
        ],
        axis=0,
    )
    ordered[...] = rhs
    for copy in copies:
        copy.wait()
    chunk = 512
    half = out_ref.shape[0] // 2
    for part in range(2):

        @pl.loop(0, half // chunk)
        def _(step):
            within = pl.ds(pl.multiple_of(step * chunk, chunk), chunk)
            rows = pl.ds(pl.multiple_of(part * half + step * chunk, chunk), chunk)
            parts = [natural(refs, within, part) for refs in x_refs]
            high, low = split(jnp.concatenate(parts, axis=1))
            full = mm(high, ordered[...])
            cols = full.shape[1] // 2
            out_ref[rows, :] = (full[:, :cols] + full[:, cols:]) + mm(low, ordered[:, :cols])


def finish(total_rows, y, gram_a, gram_b, pieces):
    operands = [chunk for piece in pieces for chunk in piece]
    rows, cols = 2 * operands[0].shape[0], operands[0].shape[1]
    return pl.pallas_call(
        functools.partial(finish_kernel, total_rows),
        out_shape=jax.ShapeDtypeStruct((rows, cols), F32),
        in_specs=[SMEM_SPEC, VMEM_SPEC, VMEM_SPEC]
        + [pl.BlockSpec(memory_space=pl.ANY)] * len(operands),
        out_specs=VMEM_SPEC,
        scratch_shapes=[
            pltpu.VMEM((NV, NV), BF),
            pltpu.VMEM((NV, NV), BF),
            pltpu.VMEM((3, cols, NV), F32),
            pltpu.VMEM((NV, 2 * cols), BF),
            pltpu.VMEM((NV, 2 * cols), BF),
            pltpu.VMEM((len(operands), rows // 2, cols), F32),
            pltpu.SemaphoreType.DMA((len(operands),)),
        ],
        compiler_params=pltpu.CompilerParams(vmem_limit_bytes=40 * 2**20),
        cost_estimate=cost(12 * 6 * cols * NV * NV, 4 * rows * cols * 9),
        name="finish",
    )(y, gram_a, gram_b, *operands)


def on_device(vectors, hamiltonian, column_blocks, live_counts, lower_bound, upper_bound):
    rows_dev, panel_cols = vectors.shape
    block_rows, slot_count, block_size, _ = hamiltonian.shape
    row_count, vec_count = lax.axis_size("row"), lax.axis_size("vec")
    first_row = lax.axis_index("row") * block_rows
    local = (column_blocks - first_row + block_rows) % (block_rows * row_count)
    live = jnp.arange(slot_count, dtype=jnp.int32)[None, :] < live_counts[:, None]
    cols = jnp.where(live, jnp.minimum(local, 3 * block_rows - 1), 3 * block_rows).reshape(-1)
    centre = (upper_bound[0] + lower_bound[0]) / 2
    radius = (upper_bound[0] - lower_bound[0]) / 2
    coef = jnp.stack([centre, 1.0 / radius])
    y = (lax.axis_index("vec") // 2)[None].astype(jnp.int32)

    def from_row(value, step):
        return lax.ppermute(value, "row", [((i + step) % row_count, i) for i in range(row_count)])

    def from_y(value, step):
        return lax.ppermute(
            value, "vec", [((i + 2 * step) % vec_count, i) for i in range(vec_count)]
        )

    def swap(value):
        return lax.ppermute(value, "vec", [(i, i ^ 1) for i in range(vec_count)])

    blocks = pack(vectors.reshape(block_rows, block_size, panel_cols))
    split_h = split_blocks(hamiltonian)

    def applied(second, operand, prev=None):
        right = from_row(operand, 1)
        left = from_row(operand, -1)
        return apply_field(second, cols, coef, split_h, left, operand, right, prev)

    own, own_s, up, up_s, down, down_s, across, across_s = ([] for _ in range(8))
    for chunk in range(CHUNKS):
        first = applied(False, blocks[chunk])
        second = applied(True, first, blocks[chunk])
        own.append(second.reshape(rows_dev // 2, panel_cols))
        up.append(from_y(own[-1], 1))
        down.append(from_y(own[-1], -1))
        own_s.append(swap(own[-1]))
        up_s.append(swap(up[-1]))
        down_s.append(swap(down[-1]))
        across.append(from_y((up, down)[chunk][-1], (1, -1)[chunk]))
        across_s.append(swap(across[-1]))
    near, lhs = gram_near((own, own_s))
    share = gram_far(y, near, lhs, (up, up_s, down))
    strip = share.shape[0] // row_count
    parts = lax.all_to_all(
        share.reshape(row_count, strip, -1), "row", split_axis=0, concat_axis=0, tiled=True
    )
    part = jnp.sum(parts, axis=0)
    groups = [
        [r * vec_count + v for r in range(row_count) for v in range(core, vec_count, 2)]
        for core in range(2)
    ]
    members = row_count * vec_count // 2
    gram_a = lax.all_to_all(
        jnp.broadcast_to(part[None], (members,) + part.shape),
        ("row", "vec"),
        split_axis=0,
        concat_axis=0,
        tiled=True,
        axis_index_groups=groups,
    ).reshape(row_count, vec_count // 2, strip, -1)
    gram_b = swap(gram_a)
    pieces = (own, own_s, up, up_s, down, down_s, across, across_s)
    return finish(rows_dev * row_count, y, gram_a, gram_b, pieces)


def solution(mesh):
    placed = (P("row", "vec"), P("row", None, None, None), P("row", None), P("row"), P(), P())

    return jax.shard_map(
        on_device, mesh=mesh, in_specs=placed, out_specs=P("row", "vec"), check_vma=False
    )
```

```python
import functools
import math

import jax
import jax.numpy as jnp
from jax import lax
from jax.experimental import pallas as pl
from jax.experimental.pallas import tpu as pltpu
from jax.sharding import PartitionSpec as P


NV = 1024
BF = jnp.bfloat16
F32 = jnp.float32


def split(x):
    high = x.astype(BF)
    return high, (x - high.astype(F32)).astype(BF)


def fold(full):
    rows, cols = full.shape[0] // 2, full.shape[1] // 2
    return (full[:rows, :cols] + full[rows:, :cols]) + (full[:rows, cols:] + full[rows:, cols:])


def mm(a, b):
    return jnp.dot(a, b, preferred_element_type=F32)


def cost(flops, moved):
    return pl.CostEstimate(flops=flops, bytes_accessed=moved, transcendentals=0)


DEPTH = 4


def split_kernel(h_ref, o_ref, buffer, arrived):
    count, size = o_ref.shape[0], h_ref.shape[-1]

    def fetch(row, slot):
        return pltpu.make_async_copy(h_ref.at[row], buffer.at[slot], arrived.at[slot])

    for slot in range(DEPTH):
        fetch(slot, slot).start()

    @pl.loop(0, count)
    def _(row):
        slot = lax.rem(row, DEPTH)
        fetch(row, slot).wait()

        @pl.loop(0, o_ref.shape[1])
        def _(k):
            high, low = split(buffer[slot, k])
            o_ref[row, k, :size, :] = high
            o_ref[row, k, size:, :] = low

        @pl.when(row + DEPTH < count)
        def _():
            fetch(row + DEPTH, slot).start()


def split_blocks(hamiltonian):
    block_rows, slots, size, _ = hamiltonian.shape
    return pl.pallas_call(
        split_kernel,
        out_shape=jax.ShapeDtypeStruct((block_rows, slots, 2 * size, size), BF),
        in_specs=[pl.BlockSpec(memory_space=pl.ANY)],
        out_specs=pl.BlockSpec(memory_space=pltpu.VMEM),
        scratch_shapes=[
            pltpu.VMEM((DEPTH, slots, size, size), F32),
            pltpu.SemaphoreType.DMA((DEPTH,)),
        ],
        compiler_params=pltpu.CompilerParams(vmem_limit_bytes=30 * 2**20),
        cost_estimate=cost(0, 8 * block_rows * slots * size * size),
        name="split_blocks",
    )(hamiltonian)


SMEM_SPEC = pl.BlockSpec(memory_space=pltpu.SMEM)
VMEM_SPEC = pl.BlockSpec(memory_space=pltpu.VMEM)


CHUNKS = 2


def lanes_low(shape):
    return lax.broadcasted_iota(jnp.int32, shape, 1) < shape[1] // 2


def turn(x):
    return pltpu.roll(x, x.shape[1] // 2, 1)


def pack_kernel(v_ref, a_ref, b_ref):
    low = lanes_low(v_ref.shape[1:])
    half = a_ref.shape[0]

    @pl.loop(0, half, unroll=2)
    def _(j):
        one, two = v_ref[j], v_ref[j + half]
        a_ref[j] = jnp.where(low, one, turn(two))
        b_ref[j] = jnp.where(low, turn(one), two)


def pack(blocks):
    count, size, cols = blocks.shape
    shape = jax.ShapeDtypeStruct((count // 2, size, cols), F32)
    return pl.pallas_call(
        pack_kernel,
        out_shape=(shape, shape),
        in_specs=[VMEM_SPEC],
        out_specs=(VMEM_SPEC, VMEM_SPEC),
        compiler_params=pltpu.CompilerParams(vmem_limit_bytes=30 * 2**20),
        cost_estimate=cost(0, 8 * blocks.size),
        name="pack",
    )(blocks)


UNROLL = 4


def field_kernel(second, cols_ref, coef_ref, h_ref, left_ref, own_ref, right_ref, *rest):
    if second:
        prev_ref, o_ref, wide = rest
    else:
        o_ref, wide = rest
    count, slots = h_ref.shape[:2]
    half = count // 2
    low = lanes_low(own_ref.shape[1:])
    for part, ref in enumerate((left_ref, own_ref, right_ref)):

        @pl.loop(0, half, unroll=2)
        def _(j):
            value = ref[j]
            high = value.astype(BF).astype(F32)
            rest_of = value - high
            wide[part * count + j] = jnp.where(low, high, turn(rest_of)).astype(BF)
            wide[part * count + half + j] = jnp.where(low, turn(high), rest_of).astype(BF)

    wide[3 * count] = jnp.zeros(wide.shape[1:], BF)
    centre, inverse = coef_ref[0], coef_ref[1]

    def row(i):
        lhs = jnp.concatenate([h_ref[i, k] for k in range(slots)], axis=1)
        rhs = jnp.concatenate([wide[cols_ref[i * slots + k]] for k in range(slots)], axis=0)
        full = mm(lhs, rhs)
        full = full[: full.shape[0] // 2] + full[full.shape[0] // 2 :]
        return full + turn(full)

    @pl.loop(0, half // UNROLL)
    def _(step):
        for within in range(UNROLL):
            i = step * UNROLL + within
            summed = jnp.where(low, row(i), row(i + half))
            result = (summed - centre * own_ref[i]) * inverse
            if second:
                result = 2.0 * result - prev_ref[i]
            o_ref[i] = result


def apply_field(second, cols, coef, split_h, left, own, right, prev=None):
    block_rows, slots, _, size = split_h.shape
    operands = [split_h, left, own, right] + ([prev] if second else [])
    return pl.pallas_call(
        functools.partial(field_kernel, second),
        out_shape=jax.ShapeDtypeStruct(own.shape, F32),
        in_specs=[SMEM_SPEC] * 2 + [VMEM_SPEC] * len(operands),
        out_specs=VMEM_SPEC,
        scratch_shapes=[pltpu.VMEM((3 * block_rows + 1, size, size), BF)],
        compiler_params=pltpu.CompilerParams(vmem_limit_bytes=30 * 2**20),
        cost_estimate=cost(8 * block_rows * slots * size**3, 2 * split_h.size),
        name="field",
    )(cols, coef, *operands)


def natural(refs, rows, part):
    a, b = (ref[rows, :] for ref in refs)
    low = lanes_low(a.shape)
    return jnp.where(low, turn(a), b) if part else jnp.where(low, a, turn(b))


GRAM_BLOCKS = 5
NEAR_BLOCKS = 2


def turned(refs, part):
    half = refs[0].shape[1] // 2
    lines = slice(part * half, (part + 1) * half)
    both = jnp.concatenate([ref[...].T[lines] for ref in refs], axis=0)
    return jnp.concatenate(split(both), axis=0)


def paired(refs, part):
    return jnp.concatenate(split(natural(refs, slice(None), part)), axis=1)


def columns_of(ref, block):
    return ref.at[:, block * 128 : (block + 1) * 128]


def near_kernel(*rest):
    own, beside = (rest[2 * n : 2 * n + 2] for n in range(2))
    out_ref, lhs = rest[4:]
    for part in range(2):
        lhs[part] = turned(own, part)
        lhs[2 + part] = turned(beside, part)
    for block, refs in enumerate((own, beside)):
        terms = [mm(lhs[part], paired(refs, part)) for part in range(2)]
        columns_of(out_ref, block)[...] = fold(terms[0] + terms[1])


def fetched(sources, held, arrived):
    copies = [
        pltpu.make_async_copy(ref, held.at[n], arrived.at[n]) for n, ref in enumerate(sources)
    ]
    for copy in copies:
        copy.start()
    return copies, [held.at[n] for n in range(len(sources))]


def far_kernel(near_ref, lhs_ref, *rest):
    out_ref, rhs, held, arrived = rest[4:]
    copies, refs = fetched(rest[:4], held, arrived)
    up, down = refs[:2], refs[2:]
    out_ref[:, : NEAR_BLOCKS * 128] = near_ref[...]
    for copy in copies[:2]:
        copy.wait()
    for part in range(2):
        rhs[part] = paired(up, part)
    for which in range(2):
        terms = [mm(lhs_ref[2 * which + part], rhs[part]) for part in range(2)]
        columns_of(out_ref, NEAR_BLOCKS + which)[...] = fold(terms[0] + terms[1])
    for copy in copies[2:]:
        copy.wait()
    terms = [mm(turned(down, part), rhs[part]) for part in range(2)]
    columns_of(out_ref, 4)[...] = fold(terms[0] + terms[1])


def flat(pieces):
    return [chunk for piece in pieces for chunk in piece]


def gram_near(pieces):
    operands = flat(pieces)
    rows, cols = operands[0].shape
    return pl.pallas_call(
        near_kernel,
        out_shape=(
            jax.ShapeDtypeStruct((cols, NEAR_BLOCKS * cols), F32),
            jax.ShapeDtypeStruct((4, 2 * cols, rows), BF),
        ),
        in_specs=[VMEM_SPEC] * len(operands),
        out_specs=(VMEM_SPEC, VMEM_SPEC),
        compiler_params=pltpu.CompilerParams(vmem_limit_bytes=30 * 2**20),
        cost_estimate=cost(32 * rows * cols * cols, 16 * rows * cols),
        name="gram_near",
    )(*operands)


def gram_far(near, lhs, pieces):
    operands = flat(pieces)
    rows, cols = operands[0].shape
    return pl.pallas_call(
        far_kernel,
        out_shape=jax.ShapeDtypeStruct((cols, GRAM_BLOCKS * cols), F32),
        in_specs=[VMEM_SPEC, VMEM_SPEC] + [pl.BlockSpec(memory_space=pl.ANY)] * len(operands),
        out_specs=VMEM_SPEC,
        scratch_shapes=[
            pltpu.VMEM((2, rows, 2 * cols), BF),
            pltpu.VMEM((len(operands), rows, cols), F32),
            pltpu.SemaphoreType.DMA((len(operands),)),
        ],
        compiler_params=pltpu.CompilerParams(vmem_limit_bytes=30 * 2**20),
        cost_estimate=cost(48 * rows * cols * cols, 24 * rows * cols),
        name="gram_far",
    )(near, lhs, *operands)


KEEP = {0: 1, 3: 2, 4: 1, 8: 1}
BASE = {2: 1, 6: 1, 10: 1, 11: 2}
PIECES = ((0, 0), (1, 0), (0, 1), (1, 1), (0, 3), (1, 3), (0, 2), (1, 2))


def finish_kernel(total_rows, y_ref, ga_ref, gb_ref, *rest):
    sources = rest[: 2 * len(PIECES)]
    out_ref, gram, gram_low, state, factor, ordered, held, arrived = rest[2 * len(PIECES) :]
    copies, held_refs = fetched(sources, held, arrived)
    x_refs = [held_refs[2 * n : 2 * n + 2] for n in range(len(PIECES))]
    grams = (ga_ref, gb_ref)
    y = y_ref[0]

    diagonal = lax.broadcasted_iota(jnp.int32, (128, 128), 0) == lax.broadcasted_iota(
        jnp.int32, (128, 128), 1
    )

    def block(k, row, b):
        return grams[k][:, row, :, b * 128 : (b + 1) * 128].reshape(128, 128)

    trace = jnp.zeros((128, 128), F32)
    for k in range(2):
        for row in range(4):
            trace += jnp.where(diagonal, block(k, row, 0), 0.0)
    energy = jnp.sum(jnp.sum(trace, axis=0, keepdims=True), axis=1, keepdims=True)
    square = NV / (4 * (energy + 1e-06))

    def put(at_row, at_col, value):
        high, low = split(value)
        rows, cols = slice(at_row * 128, at_row * 128 + 128), slice(at_col * 128, at_col * 128 + 128)
        gram[rows, cols] = high
        gram_low[rows, cols] = low

    for k in range(2):
        for row in range(4):
            here = 4 * k + row
            after, before = (row + 1) % 4, (row + 3) % 4
            side = k if row < 2 else 1 - k
            put(here, here, block(k, row, 0) * square)
            put(here, 4 * (1 - k) + row, block(k, row, 1) * square)
            for one, two, b in (
                (here, 4 * k + after, 2),
                (4 * (1 - k) + row, 4 * k + after, 3),
                (4 * side + before, 4 * k + after, 4),
            ):
                value = block(k, row, b) * square
                put(one, two, value)
                put(two, one, value.T)

    mine = pl.ds(pl.multiple_of(y * 128, 128), 128)
    column = lax.broadcasted_iota(jnp.int32, (128, NV), 1) - y * 128
    unit = (column == lax.broadcasted_iota(jnp.int32, (128, NV), 0)).astype(F32)
    state[0] = 1.5 * unit - 0.5 * (gram[mine, :].astype(F32) + gram_low[mine, :].astype(F32))

    @pl.loop(0, 12)
    def _(step):
        current = state[0]
        for at, slot in KEEP.items():

            @pl.when(step == at)
            def _():
                state[slot] = current

        slot = jnp.int32(0)
        for at, value in BASE.items():
            slot = jnp.where(step == at, value, slot)
        high, low = split(current)
        twice = mm(jnp.concatenate([high, low], axis=0), gram[...])
        product = (twice[:128] + twice[128:]) + mm(high, gram_low[...])
        state[0] = 1.5 * state[slot] - 0.5 * product

    scale = jnp.sqrt(square) * math.sqrt(total_rows)
    high, low = split(state[0].T * scale)
    factor[:, :128] = high
    factor[:, 128:] = low

    def core(k, dy):
        return jnp.where(y < 2, k, 1 - k) if dy == 3 else k

    rhs = jnp.concatenate(
        [
            factor[pl.ds(pl.multiple_of((4 * core(k, dy) + lax.rem(y + dy, 4)) * 128, 128), 128), :]
            for k, dy in PIECES
        ],
        axis=0,
    )
    ordered[...] = rhs
    for copy in copies:
        copy.wait()
    chunk = 512
    half = out_ref.shape[0] // 2
    for part in range(2):

        @pl.loop(0, half // chunk)
        def _(step):
            within = pl.ds(pl.multiple_of(step * chunk, chunk), chunk)
            rows = pl.ds(pl.multiple_of(part * half + step * chunk, chunk), chunk)
            parts = [natural(refs, within, part) for refs in x_refs]
            high, low = split(jnp.concatenate(parts, axis=1))
            full = mm(high, ordered[...])
            cols = full.shape[1] // 2
            out_ref[rows, :] = (full[:, :cols] + full[:, cols:]) + mm(low, ordered[:, :cols])


def finish(total_rows, y, gram_a, gram_b, pieces):
    operands = [chunk for piece in pieces for chunk in piece]
    rows, cols = 2 * operands[0].shape[0], operands[0].shape[1]
    return pl.pallas_call(
        functools.partial(finish_kernel, total_rows),
        out_shape=jax.ShapeDtypeStruct((rows, cols), F32),
        in_specs=[SMEM_SPEC, VMEM_SPEC, VMEM_SPEC]
        + [pl.BlockSpec(memory_space=pl.ANY)] * len(operands),
        out_specs=VMEM_SPEC,
        scratch_shapes=[
            pltpu.VMEM((NV, NV), BF),
            pltpu.VMEM((NV, NV), BF),
            pltpu.VMEM((3, cols, NV), F32),
            pltpu.VMEM((NV, 2 * cols), BF),
            pltpu.VMEM((NV, 2 * cols), BF),
            pltpu.VMEM((len(operands), rows // 2, cols), F32),
            pltpu.SemaphoreType.DMA((len(operands),)),
        ],
        compiler_params=pltpu.CompilerParams(vmem_limit_bytes=40 * 2**20),
        cost_estimate=cost(12 * 6 * cols * NV * NV, 4 * rows * cols * 9),
        name="finish",
    )(y, gram_a, gram_b, *operands)


def on_device(vectors, hamiltonian, column_blocks, live_counts, lower_bound, upper_bound):
    rows_dev, panel_cols = vectors.shape
    block_rows, slot_count, block_size, _ = hamiltonian.shape
    row_count, vec_count = lax.axis_size("row"), lax.axis_size("vec")
    first_row = lax.axis_index("row") * block_rows
    local = (column_blocks - first_row + block_rows) % (block_rows * row_count)
    live = jnp.arange(slot_count, dtype=jnp.int32)[None, :] < live_counts[:, None]
    cols = jnp.where(live, jnp.minimum(local, 3 * block_rows - 1), 3 * block_rows).reshape(-1)
    centre = (upper_bound[0] + lower_bound[0]) / 2
    radius = (upper_bound[0] - lower_bound[0]) / 2
    coef = jnp.stack([centre, 1.0 / radius])
    y = (lax.axis_index("vec") // 2)[None].astype(jnp.int32)

    def from_row(value, step):
        return lax.ppermute(value, "row", [((i + step) % row_count, i) for i in range(row_count)])

    def from_y(value, step):
        return lax.ppermute(
            value, "vec", [((i + 2 * step) % vec_count, i) for i in range(vec_count)]
        )

    def from_last(value):
        return lax.ppermute(
            value, "vec", [((i - 2) % vec_count ^ (i >= 4), i) for i in range(vec_count)]
        )

    def swap(value):
        return lax.ppermute(value, "vec", [(i, i ^ 1) for i in range(vec_count)])

    def across_last(value):
        sources = [(i - 2) % vec_count for i in range(vec_count)]
        return lax.ppermute(value, "vec", [(s ^ (s >= 4), i) for i, s in enumerate(sources)])

    blocks = pack(vectors.reshape(block_rows, block_size, panel_cols))
    split_h = split_blocks(hamiltonian)

    def applied(second, operand, prev=None):
        right = from_row(operand, 1)
        left = from_row(operand, -1)
        return apply_field(second, cols, coef, split_h, left, operand, right, prev)

    own, own_s, up, up_s, down, down_s, across, across_s = ([] for _ in range(8))
    for chunk in range(CHUNKS):
        first = applied(False, blocks[chunk])
        second = applied(True, first, blocks[chunk])
        own.append(second.reshape(rows_dev // 2, panel_cols))
        up.append(from_y(own[-1], 1))
        down.append(from_last(own[-1]))
        own_s.append(swap(own[-1]))
        up_s.append(swap(up[-1]))
        down_s.append(swap(down[-1]))
        across.append(across_last(down[-1]) if chunk else from_y(up[-1], 1))
        across_s.append(swap(across[-1]))
    near, lhs = gram_near((own, own_s))
    share = gram_far(near, lhs, (up, down))
    strip = share.shape[0] // row_count
    parts = lax.all_to_all(
        share.reshape(row_count, strip, -1), "row", split_axis=0, concat_axis=0, tiled=True
    )
    part = jnp.sum(parts, axis=0)
    groups = [
        [r * vec_count + v for r in range(row_count) for v in range(core, vec_count, 2)]
        for core in range(2)
    ]
    members = row_count * vec_count // 2
    gram_a = lax.all_to_all(
        jnp.broadcast_to(part[None], (members,) + part.shape),
        ("row", "vec"),
        split_axis=0,
        concat_axis=0,
        tiled=True,
        axis_index_groups=groups,
    ).reshape(row_count, vec_count // 2, strip, -1)
    gram_b = swap(gram_a)
    pieces = (own, own_s, up, up_s, down, down_s, across, across_s)
    return finish(rows_dev * row_count, y, gram_a, gram_b, pieces)


def solution(mesh):
    placed = (P("row", "vec"), P("row", None, None, None), P("row", None), P("row"), P(), P())

    return jax.shard_map(
        on_device, mesh=mesh, in_specs=placed, out_specs=P("row", "vec"), check_vma=False
    )
```

```python
import functools
import math

import jax
import jax.numpy as jnp
from jax import lax
from jax.experimental import pallas as pl
from jax.experimental.pallas import tpu as pltpu
from jax.sharding import PartitionSpec as P


NV = 1024
BF = jnp.bfloat16
F32 = jnp.float32


def split(x):
    high = x.astype(BF)
    return high, (x - high.astype(F32)).astype(BF)


def fold(full):
    rows, cols = full.shape[0] // 2, full.shape[1] // 2
    return (full[:rows, :cols] + full[rows:, :cols]) + (full[:rows, cols:] + full[rows:, cols:])


def mm(a, b):
    return jnp.dot(a, b, preferred_element_type=F32)


def cost(flops, moved):
    return pl.CostEstimate(flops=flops, bytes_accessed=moved, transcendentals=0)


DEPTH = 4


def split_kernel(h_ref, o_ref, buffer, arrived):
    count, size = o_ref.shape[0], h_ref.shape[-1]

    def fetch(row, slot):
        return pltpu.make_async_copy(h_ref.at[row], buffer.at[slot], arrived.at[slot])

    for slot in range(DEPTH):
        fetch(slot, slot).start()

    @pl.loop(0, count)
    def _(row):
        slot = lax.rem(row, DEPTH)
        fetch(row, slot).wait()

        @pl.loop(0, o_ref.shape[1])
        def _(k):
            high, low = split(buffer[slot, k])
            o_ref[row, k, :size, :] = high
            o_ref[row, k, size:, :] = low

        @pl.when(row + DEPTH < count)
        def _():
            fetch(row + DEPTH, slot).start()


def split_blocks(hamiltonian):
    block_rows, slots, size, _ = hamiltonian.shape
    return pl.pallas_call(
        split_kernel,
        out_shape=jax.ShapeDtypeStruct((block_rows, slots, 2 * size, size), BF),
        in_specs=[pl.BlockSpec(memory_space=pl.ANY)],
        out_specs=pl.BlockSpec(memory_space=pltpu.VMEM),
        scratch_shapes=[
            pltpu.VMEM((DEPTH, slots, size, size), F32),
            pltpu.SemaphoreType.DMA((DEPTH,)),
        ],
        compiler_params=pltpu.CompilerParams(vmem_limit_bytes=30 * 2**20),
        cost_estimate=cost(0, 8 * block_rows * slots * size * size),
        name="split_blocks",
    )(hamiltonian)


SMEM_SPEC = pl.BlockSpec(memory_space=pltpu.SMEM)
VMEM_SPEC = pl.BlockSpec(memory_space=pltpu.VMEM)


CHUNKS = 2


def lanes_low(shape):
    return lax.broadcasted_iota(jnp.int32, shape, 1) < shape[1] // 2


def turn(x):
    return pltpu.roll(x, x.shape[1] // 2, 1)


def pack_kernel(v_ref, a_ref, b_ref):
    low = lanes_low(v_ref.shape[1:])
    half = a_ref.shape[0]

    @pl.loop(0, half, unroll=2)
    def _(j):
        one, two = v_ref[j], v_ref[j + half]
        a_ref[j] = jnp.where(low, one, turn(two))
        b_ref[j] = jnp.where(low, turn(one), two)


def pack(blocks):
    count, size, cols = blocks.shape
    shape = jax.ShapeDtypeStruct((count // 2, size, cols), F32)
    return pl.pallas_call(
        pack_kernel,
        out_shape=(shape, shape),
        in_specs=[VMEM_SPEC],
        out_specs=(VMEM_SPEC, VMEM_SPEC),
        compiler_params=pltpu.CompilerParams(vmem_limit_bytes=30 * 2**20),
        cost_estimate=cost(0, 8 * blocks.size),
        name="pack",
    )(blocks)


UNROLL = 4


def field_kernel(second, cols_ref, coef_ref, h_ref, left_ref, own_ref, right_ref, *rest):
    if second:
        prev_ref, o_ref, wide = rest
    else:
        o_ref, wide = rest
    count, slots = h_ref.shape[:2]
    half = count // 2
    low = lanes_low(own_ref.shape[1:])
    for part, ref in enumerate((left_ref, own_ref, right_ref)):

        @pl.loop(0, half, unroll=2)
        def _(j):
            value = ref[j]
            high = value.astype(BF).astype(F32)
            rest_of = value - high
            wide[part * count + j] = jnp.where(low, high, turn(rest_of)).astype(BF)
            wide[part * count + half + j] = jnp.where(low, turn(high), rest_of).astype(BF)

    wide[3 * count] = jnp.zeros(wide.shape[1:], BF)
    centre, inverse = coef_ref[0], coef_ref[1]

    def row(i):
        lhs = jnp.concatenate([h_ref[i, k] for k in range(slots)], axis=1)
        rhs = jnp.concatenate([wide[cols_ref[i * slots + k]] for k in range(slots)], axis=0)
        full = mm(lhs, rhs)
        full = full[: full.shape[0] // 2] + full[full.shape[0] // 2 :]
        return full + turn(full)

    @pl.loop(0, half // UNROLL)
    def _(step):
        for within in range(UNROLL):
            i = step * UNROLL + within
            summed = jnp.where(low, row(i), row(i + half))
            result = (summed - centre * own_ref[i]) * inverse
            if second:
                result = 2.0 * result - prev_ref[i]
            o_ref[i] = result


def apply_field(second, cols, coef, split_h, left, own, right, prev=None):
    block_rows, slots, _, size = split_h.shape
    operands = [split_h, left, own, right] + ([prev] if second else [])
    return pl.pallas_call(
        functools.partial(field_kernel, second),
        out_shape=jax.ShapeDtypeStruct(own.shape, F32),
        in_specs=[SMEM_SPEC] * 2 + [VMEM_SPEC] * len(operands),
        out_specs=VMEM_SPEC,
        scratch_shapes=[pltpu.VMEM((3 * block_rows + 1, size, size), BF)],
        compiler_params=pltpu.CompilerParams(vmem_limit_bytes=30 * 2**20),
        cost_estimate=cost(8 * block_rows * slots * size**3, 2 * split_h.size),
        name="field",
    )(cols, coef, *operands)


def natural(refs, rows, part):
    a, b = (ref[rows, :] for ref in refs)
    low = lanes_low(a.shape)
    return jnp.where(low, turn(a), b) if part else jnp.where(low, a, turn(b))


GRAM_BLOCKS = 5
NEAR_BLOCKS = 2


def turned(refs, part):
    half = refs[0].shape[1] // 2
    lines = slice(part * half, (part + 1) * half)
    both = jnp.concatenate([ref[...].T[lines] for ref in refs], axis=0)
    return jnp.concatenate(split(both), axis=0)


def paired(refs, part):
    return jnp.concatenate(split(natural(refs, slice(None), part)), axis=1)


def columns_of(ref, block):
    return ref.at[:, block * 128 : (block + 1) * 128]


def near_kernel(*rest):
    own, beside = (rest[2 * n : 2 * n + 2] for n in range(2))
    out_ref, lhs = rest[4:]
    for part in range(2):
        lhs[part] = turned(own, part)
        lhs[2 + part] = turned(beside, part)
    for block, refs in enumerate((own, beside)):
        terms = [mm(lhs[part], paired(refs, part)) for part in range(2)]
        columns_of(out_ref, block)[...] = fold(terms[0] + terms[1])


def fetched(sources, held, arrived):
    copies = [
        pltpu.make_async_copy(ref, held.at[n], arrived.at[n]) for n, ref in enumerate(sources)
    ]
    for copy in copies:
        copy.start()
    return copies, [held.at[n] for n in range(len(sources))]


def far_kernel(near_ref, lhs_ref, *rest):
    out_ref, rhs, held, arrived = rest[4:]
    copies, refs = fetched(rest[:4], held, arrived)
    up, down = refs[:2], refs[2:]
    out_ref[:, : NEAR_BLOCKS * 128] = near_ref[...]
    for copy in copies[:2]:
        copy.wait()
    for part in range(2):
        rhs[part] = paired(up, part)
    for which in range(2):
        terms = [mm(lhs_ref[2 * which + part], rhs[part]) for part in range(2)]
        columns_of(out_ref, NEAR_BLOCKS + which)[...] = fold(terms[0] + terms[1])
    for copy in copies[2:]:
        copy.wait()
    terms = [mm(turned(down, part), rhs[part]) for part in range(2)]
    columns_of(out_ref, 4)[...] = fold(terms[0] + terms[1])


def flat(pieces):
    return [chunk for piece in pieces for chunk in piece]


def gram_near(pieces):
    operands = flat(pieces)
    rows, cols = operands[0].shape
    return pl.pallas_call(
        near_kernel,
        out_shape=(
            jax.ShapeDtypeStruct((cols, NEAR_BLOCKS * cols), F32),
            jax.ShapeDtypeStruct((4, 2 * cols, rows), BF),
        ),
        in_specs=[VMEM_SPEC] * len(operands),
        out_specs=(VMEM_SPEC, VMEM_SPEC),
        compiler_params=pltpu.CompilerParams(vmem_limit_bytes=30 * 2**20),
        cost_estimate=cost(32 * rows * cols * cols, 16 * rows * cols),
        name="gram_near",
    )(*operands)


def gram_far(near, lhs, pieces):
    operands = flat(pieces)
    rows, cols = operands[0].shape
    return pl.pallas_call(
        far_kernel,
        out_shape=jax.ShapeDtypeStruct((cols, GRAM_BLOCKS * cols), F32),
        in_specs=[VMEM_SPEC, VMEM_SPEC] + [pl.BlockSpec(memory_space=pl.ANY)] * len(operands),
        out_specs=VMEM_SPEC,
        scratch_shapes=[
            pltpu.VMEM((2, rows, 2 * cols), BF),
            pltpu.VMEM((len(operands), rows, cols), F32),
            pltpu.SemaphoreType.DMA((len(operands),)),
        ],
        compiler_params=pltpu.CompilerParams(vmem_limit_bytes=30 * 2**20),
        cost_estimate=cost(48 * rows * cols * cols, 24 * rows * cols),
        name="gram_far",
    )(near, lhs, *operands)


def total_kernel(parts_ref, out_ref):
    total = parts_ref[0]
    for n in range(1, parts_ref.shape[0]):
        total += parts_ref[n]

    @pl.loop(0, out_ref.shape[0], unroll=4)
    def _(n):
        out_ref[n] = total


def strip_total(parts, copies):
    return pl.pallas_call(
        total_kernel,
        out_shape=jax.ShapeDtypeStruct((copies,) + parts.shape[1:], F32),
        in_specs=[VMEM_SPEC],
        out_specs=VMEM_SPEC,
        compiler_params=pltpu.CompilerParams(vmem_limit_bytes=8 * 2**20),
        cost_estimate=cost(parts.size, 8 * parts.size),
        name="total",
    )(parts)


KEEP = {0: 1, 3: 2, 4: 1, 8: 1}
BASE = {2: 1, 6: 1, 10: 1, 11: 2}
PIECES = ((0, 0), (1, 0), (0, 1), (1, 1), (0, 3), (1, 3), (0, 2), (1, 2))


def finish_kernel(total_rows, y_ref, ga_ref, gb_ref, *rest):
    sources = rest[: 2 * len(PIECES)]
    out_ref, gram, gram_low, state, factor, ordered, held, arrived = rest[2 * len(PIECES) :]
    copies, held_refs = fetched(sources, held, arrived)
    x_refs = [held_refs[2 * n : 2 * n + 2] for n in range(len(PIECES))]
    grams = (ga_ref, gb_ref)
    y = y_ref[0]

    diagonal = lax.broadcasted_iota(jnp.int32, (128, 128), 0) == lax.broadcasted_iota(
        jnp.int32, (128, 128), 1
    )

    def block(k, row, b):
        return grams[k][:, row, :, b * 128 : (b + 1) * 128].reshape(128, 128)

    trace = jnp.zeros((128, 128), F32)
    for k in range(2):
        for row in range(4):
            trace += jnp.where(diagonal, block(k, row, 0), 0.0)
    energy = jnp.sum(jnp.sum(trace, axis=0, keepdims=True), axis=1, keepdims=True)
    square = NV / (4 * (energy + 1e-06))

    def put(at_row, at_col, value):
        high, low = split(value)
        rows, cols = slice(at_row * 128, at_row * 128 + 128), slice(at_col * 128, at_col * 128 + 128)
        gram[rows, cols] = high
        gram_low[rows, cols] = low

    for k in range(2):
        for row in range(4):
            here = 4 * k + row
            after, before = (row + 1) % 4, (row + 3) % 4
            side = k if row < 2 else 1 - k
            put(here, here, block(k, row, 0) * square)
            put(here, 4 * (1 - k) + row, block(k, row, 1) * square)
            for one, two, b in (
                (here, 4 * k + after, 2),
                (4 * (1 - k) + row, 4 * k + after, 3),
                (4 * side + before, 4 * k + after, 4),
            ):
                value = block(k, row, b) * square
                put(one, two, value)
                put(two, one, value.T)

    mine = pl.ds(pl.multiple_of(y * 128, 128), 128)
    column = lax.broadcasted_iota(jnp.int32, (128, NV), 1) - y * 128
    unit = (column == lax.broadcasted_iota(jnp.int32, (128, NV), 0)).astype(F32)
    state[0] = 1.5 * unit - 0.5 * (gram[mine, :].astype(F32) + gram_low[mine, :].astype(F32))

    @pl.loop(0, 12)
    def _(step):
        current = state[0]
        for at, slot in KEEP.items():

            @pl.when(step == at)
            def _():
                state[slot] = current

        slot = jnp.int32(0)
        for at, value in BASE.items():
            slot = jnp.where(step == at, value, slot)
        high, low = split(current)
        twice = mm(jnp.concatenate([high, low], axis=0), gram[...])
        product = (twice[:128] + twice[128:]) + mm(high, gram_low[...])
        state[0] = 1.5 * state[slot] - 0.5 * product

    scale = jnp.sqrt(square) * math.sqrt(total_rows)
    high, low = split(state[0].T * scale)
    factor[:, :128] = high
    factor[:, 128:] = low

    def core(k, dy):
        return jnp.where(y < 2, k, 1 - k) if dy == 3 else k

    rhs = jnp.concatenate(
        [
            factor[pl.ds(pl.multiple_of((4 * core(k, dy) + lax.rem(y + dy, 4)) * 128, 128), 128), :]
            for k, dy in PIECES
        ],
        axis=0,
    )
    ordered[...] = rhs
    for copy in copies:
        copy.wait()
    chunk = 512
    half = out_ref.shape[0] // 2
    for part in range(2):

        @pl.loop(0, half // chunk)
        def _(step):
            within = pl.ds(pl.multiple_of(step * chunk, chunk), chunk)
            rows = pl.ds(pl.multiple_of(part * half + step * chunk, chunk), chunk)
            parts = [natural(refs, within, part) for refs in x_refs]
            high, low = split(jnp.concatenate(parts, axis=1))
            full = mm(high, ordered[...])
            cols = full.shape[1] // 2
            out_ref[rows, :] = (full[:, :cols] + full[:, cols:]) + mm(low, ordered[:, :cols])


def finish(total_rows, y, gram_a, gram_b, pieces):
    operands = [chunk for piece in pieces for chunk in piece]
    rows, cols = 2 * operands[0].shape[0], operands[0].shape[1]
    return pl.pallas_call(
        functools.partial(finish_kernel, total_rows),
        out_shape=jax.ShapeDtypeStruct((rows, cols), F32),
        in_specs=[SMEM_SPEC, VMEM_SPEC, VMEM_SPEC]
        + [pl.BlockSpec(memory_space=pltpu.HBM)] * len(operands),
        out_specs=VMEM_SPEC,
        scratch_shapes=[
            pltpu.VMEM((NV, NV), BF),
            pltpu.VMEM((NV, NV), BF),
            pltpu.VMEM((3, cols, NV), F32),
            pltpu.VMEM((NV, 2 * cols), BF),
            pltpu.VMEM((NV, 2 * cols), BF),
            pltpu.VMEM((len(operands), rows // 2, cols), F32),
            pltpu.SemaphoreType.DMA((len(operands),)),
        ],
        compiler_params=pltpu.CompilerParams(vmem_limit_bytes=40 * 2**20),
        cost_estimate=cost(12 * 6 * cols * NV * NV, 4 * rows * cols * 9),
        name="finish",
    )(y, gram_a, gram_b, *operands)


def on_device(vectors, hamiltonian, column_blocks, live_counts, lower_bound, upper_bound):
    rows_dev, panel_cols = vectors.shape
    block_rows, slot_count, block_size, _ = hamiltonian.shape
    row_count, vec_count = lax.axis_size("row"), lax.axis_size("vec")
    first_row = lax.axis_index("row") * block_rows
    local = (column_blocks - first_row + block_rows) % (block_rows * row_count)
    live = jnp.arange(slot_count, dtype=jnp.int32)[None, :] < live_counts[:, None]
    cols = jnp.where(live, jnp.minimum(local, 3 * block_rows - 1), 3 * block_rows).reshape(-1)
    centre = (upper_bound[0] + lower_bound[0]) / 2
    radius = (upper_bound[0] - lower_bound[0]) / 2
    coef = jnp.stack([centre, 1.0 / radius])
    y = (lax.axis_index("vec") // 2)[None].astype(jnp.int32)

    def from_row(value, step):
        return lax.ppermute(value, "row", [((i + step) % row_count, i) for i in range(row_count)])

    def from_y(value, step):
        return lax.ppermute(
            value, "vec", [((i + 2 * step) % vec_count, i) for i in range(vec_count)]
        )

    def from_last(value):
        return lax.ppermute(
            value, "vec", [((i - 2) % vec_count ^ (i >= 4), i) for i in range(vec_count)]
        )

    def swap(value):
        return lax.ppermute(value, "vec", [(i, i ^ 1) for i in range(vec_count)])

    def across_last(value):
        sources = [(i - 2) % vec_count for i in range(vec_count)]
        return lax.ppermute(value, "vec", [(s ^ (s >= 4), i) for i, s in enumerate(sources)])

    blocks = pack(vectors.reshape(block_rows, block_size, panel_cols))
    split_h = split_blocks(hamiltonian)

    def applied(second, operand, prev=None):
        right = from_row(operand, 1)
        left = from_row(operand, -1)
        return apply_field(second, cols, coef, split_h, left, operand, right, prev)

    own, beside, own_s, up, up_s, down, down_s, across, across_s = ([] for _ in range(9))
    for chunk in range(CHUNKS):
        first = applied(False, blocks[chunk])
        second = applied(True, first, blocks[chunk])
        own.append(second.reshape(rows_dev // 2, panel_cols))
        up.append(from_y(own[-1], 1))
        down.append(from_last(own[-1]))
        beside.append(swap(own[-1]))
        own_s.append(swap(lax.optimization_barrier(own[-1])))
        up_s.append(swap(up[-1]))
        down_s.append(swap(down[-1]))
        across.append(across_last(down[-1]) if chunk else from_y(up[-1], 1))
        across_s.append(swap(across[-1]))
    near, lhs = gram_near((own, beside))
    share = gram_far(near, lhs, (up, down))
    strip = share.shape[0] // row_count
    parts = lax.all_to_all(
        share.reshape(row_count, strip, -1), "row", split_axis=0, concat_axis=0, tiled=True
    )
    groups = [
        [r * vec_count + v for r in range(row_count) for v in range(core, vec_count, 2)]
        for core in range(2)
    ]
    members = row_count * vec_count // 2
    part = strip_total(parts, members)
    gram_a = lax.all_to_all(
        part,
        ("row", "vec"),
        split_axis=0,
        concat_axis=0,
        tiled=True,
        axis_index_groups=groups,
    ).reshape(row_count, vec_count // 2, strip, -1)
    gram_b = swap(gram_a)
    pieces = (own, own_s, up, up_s, down, down_s, across, across_s)
    return finish(rows_dev * row_count, y, gram_a, gram_b, pieces)


def solution(mesh):
    placed = (P("row", "vec"), P("row", None, None, None), P("row", None), P("row"), P(), P())

    return jax.shard_map(
        on_device, mesh=mesh, in_specs=placed, out_specs=P("row", "vec"), check_vma=False
    )
```

```python
import functools
import math

import jax
import jax.numpy as jnp
from jax import lax
from jax.experimental import pallas as pl
from jax.experimental.pallas import tpu as pltpu
from jax.sharding import PartitionSpec as P


NV = 1024
BF = jnp.bfloat16
F32 = jnp.float32


def split(x):
    high = x.astype(BF)
    return high, (x - high.astype(F32)).astype(BF)


def fold(full):
    rows, cols = full.shape[0] // 2, full.shape[1] // 2
    return (full[:rows, :cols] + full[rows:, :cols]) + (full[:rows, cols:] + full[rows:, cols:])


def mm(a, b):
    return jnp.dot(a, b, preferred_element_type=F32)


def cost(flops, moved):
    return pl.CostEstimate(flops=flops, bytes_accessed=moved, transcendentals=0)


DEPTH = 4


def split_kernel(h_ref, o_ref, buffer, arrived):
    count, size = o_ref.shape[0], h_ref.shape[-1]

    def fetch(row, slot):
        return pltpu.make_async_copy(h_ref.at[row], buffer.at[slot], arrived.at[slot])

    for slot in range(DEPTH):
        fetch(slot, slot).start()

    @pl.loop(0, count)
    def _(row):
        slot = lax.rem(row, DEPTH)
        fetch(row, slot).wait()

        @pl.loop(0, o_ref.shape[1])
        def _(k):
            high, low = split(buffer[slot, k])
            o_ref[row, k, :size, :] = high
            o_ref[row, k, size:, :] = low

        @pl.when(row + DEPTH < count)
        def _():
            fetch(row + DEPTH, slot).start()


def split_blocks(hamiltonian):
    block_rows, slots, size, _ = hamiltonian.shape
    return pl.pallas_call(
        split_kernel,
        out_shape=jax.ShapeDtypeStruct((block_rows, slots, 2 * size, size), BF),
        in_specs=[pl.BlockSpec(memory_space=pl.ANY)],
        out_specs=pl.BlockSpec(memory_space=pltpu.VMEM),
        scratch_shapes=[
            pltpu.VMEM((DEPTH, slots, size, size), F32),
            pltpu.SemaphoreType.DMA((DEPTH,)),
        ],
        compiler_params=pltpu.CompilerParams(vmem_limit_bytes=30 * 2**20),
        cost_estimate=cost(0, 8 * block_rows * slots * size * size),
        name="split_blocks",
    )(hamiltonian)


SMEM_SPEC = pl.BlockSpec(memory_space=pltpu.SMEM)
VMEM_SPEC = pl.BlockSpec(memory_space=pltpu.VMEM)


CHUNKS = 2


def lanes_low(shape):
    return lax.broadcasted_iota(jnp.int32, shape, 1) < shape[1] // 2


def turn(x):
    return pltpu.roll(x, x.shape[1] // 2, 1)


def pack_kernel(v_ref, a_ref, b_ref):
    low = lanes_low(v_ref.shape[1:])
    half = a_ref.shape[0]

    @pl.loop(0, half, unroll=2)
    def _(j):
        one, two = v_ref[j], v_ref[j + half]
        a_ref[j] = jnp.where(low, one, turn(two))
        b_ref[j] = jnp.where(low, turn(one), two)


def pack(blocks):
    count, size, cols = blocks.shape
    shape = jax.ShapeDtypeStruct((count // 2, size, cols), F32)
    return pl.pallas_call(
        pack_kernel,
        out_shape=(shape, shape),
        in_specs=[VMEM_SPEC],
        out_specs=(VMEM_SPEC, VMEM_SPEC),
        compiler_params=pltpu.CompilerParams(vmem_limit_bytes=30 * 2**20),
        cost_estimate=cost(0, 8 * blocks.size),
        name="pack",
    )(blocks)


UNROLL = 4


def field_kernel(second, cols_ref, coef_ref, h_ref, left_ref, own_ref, right_ref, *rest):
    if second:
        prev_ref, o_ref, wide = rest
    else:
        o_ref, wide = rest
    count, slots = h_ref.shape[:2]
    half = count // 2
    low = lanes_low(own_ref.shape[1:])
    for part, ref in enumerate((left_ref, own_ref, right_ref)):

        @pl.loop(0, half, unroll=2)
        def _(j):
            value = ref[j]
            high = value.astype(BF).astype(F32)
            rest_of = value - high
            wide[part * count + j] = jnp.where(low, high, turn(rest_of)).astype(BF)
            wide[part * count + half + j] = jnp.where(low, turn(high), rest_of).astype(BF)

    wide[3 * count] = jnp.zeros(wide.shape[1:], BF)
    centre, inverse = coef_ref[0], coef_ref[1]

    def row(i):
        lhs = jnp.concatenate([h_ref[i, k] for k in range(slots)], axis=1)
        rhs = jnp.concatenate([wide[cols_ref[i * slots + k]] for k in range(slots)], axis=0)
        full = mm(lhs, rhs)
        full = full[: full.shape[0] // 2] + full[full.shape[0] // 2 :]
        return full + turn(full)

    @pl.loop(0, half // UNROLL)
    def _(step):
        for within in range(UNROLL):
            i = step * UNROLL + within
            summed = jnp.where(low, row(i), row(i + half))
            result = (summed - centre * own_ref[i]) * inverse
            if second:
                result = 2.0 * result - prev_ref[i]
            o_ref[i] = result


def apply_field(second, cols, coef, split_h, left, own, right, prev=None):
    block_rows, slots, _, size = split_h.shape
    operands = [split_h, left, own, right] + ([prev] if second else [])
    return pl.pallas_call(
        functools.partial(field_kernel, second),
        out_shape=jax.ShapeDtypeStruct(own.shape, F32),
        in_specs=[SMEM_SPEC] * 2 + [VMEM_SPEC] * len(operands),
        out_specs=VMEM_SPEC,
        scratch_shapes=[pltpu.VMEM((3 * block_rows + 1, size, size), BF)],
        compiler_params=pltpu.CompilerParams(vmem_limit_bytes=30 * 2**20),
        cost_estimate=cost(8 * block_rows * slots * size**3, 2 * split_h.size),
        name="field",
    )(cols, coef, *operands)


def natural(refs, rows, part):
    a, b = (ref[rows, :] for ref in refs)
    low = lanes_low(a.shape)
    return jnp.where(low, turn(a), b) if part else jnp.where(low, a, turn(b))


GRAM_BLOCKS = 5
NEAR_BLOCKS = 2


def turned(refs, part):
    half = refs[0].shape[1] // 2
    lines = slice(part * half, (part + 1) * half)
    both = jnp.concatenate([ref[...].T[lines] for ref in refs], axis=0)
    return jnp.concatenate(split(both), axis=0)


def paired(refs, part):
    return jnp.concatenate(split(natural(refs, slice(None), part)), axis=1)


def columns_of(ref, block):
    return ref.at[:, block * 128 : (block + 1) * 128]


def near_kernel(*rest):
    own, beside = (rest[2 * n : 2 * n + 2] for n in range(2))
    out_ref, lhs = rest[4:]
    for part in range(2):
        lhs[part] = turned(own, part)
        lhs[2 + part] = turned(beside, part)
    for block, refs in enumerate((own, beside)):
        terms = [mm(lhs[part], paired(refs, part)) for part in range(2)]
        columns_of(out_ref, block)[...] = fold(terms[0] + terms[1])


def fetched(sources, held, arrived):
    copies = [
        pltpu.make_async_copy(ref, held.at[n], arrived.at[n]) for n, ref in enumerate(sources)
    ]
    for copy in copies:
        copy.start()
    return copies, [held.at[n] for n in range(len(sources))]


def far_kernel(near_ref, lhs_ref, *rest):
    out_ref, rhs, held, arrived = rest[4:]
    copies, refs = fetched(rest[:4], held, arrived)
    up, down = refs[:2], refs[2:]
    out_ref[:, : NEAR_BLOCKS * 128] = near_ref[...]
    for copy in copies[:2]:
        copy.wait()
    for part in range(2):
        rhs[part] = paired(up, part)
    for which in range(2):
        terms = [mm(lhs_ref[2 * which + part], rhs[part]) for part in range(2)]
        columns_of(out_ref, NEAR_BLOCKS + which)[...] = fold(terms[0] + terms[1])
    for copy in copies[2:]:
        copy.wait()
    terms = [mm(turned(down, part), rhs[part]) for part in range(2)]
    columns_of(out_ref, 4)[...] = fold(terms[0] + terms[1])


def flat(pieces):
    return [chunk for piece in pieces for chunk in piece]


def gram_near(pieces):
    operands = flat(pieces)
    rows, cols = operands[0].shape
    return pl.pallas_call(
        near_kernel,
        out_shape=(
            jax.ShapeDtypeStruct((cols, NEAR_BLOCKS * cols), F32),
            jax.ShapeDtypeStruct((4, 2 * cols, rows), BF),
        ),
        in_specs=[VMEM_SPEC] * len(operands),
        out_specs=(VMEM_SPEC, VMEM_SPEC),
        compiler_params=pltpu.CompilerParams(vmem_limit_bytes=30 * 2**20),
        cost_estimate=cost(32 * rows * cols * cols, 16 * rows * cols),
        name="gram_near",
    )(*operands)


def gram_far(near, lhs, pieces):
    operands = flat(pieces)
    rows, cols = operands[0].shape
    return pl.pallas_call(
        far_kernel,
        out_shape=jax.ShapeDtypeStruct((cols, GRAM_BLOCKS * cols), F32),
        in_specs=[VMEM_SPEC, VMEM_SPEC] + [pl.BlockSpec(memory_space=pl.ANY)] * len(operands),
        out_specs=VMEM_SPEC,
        scratch_shapes=[
            pltpu.VMEM((2, rows, 2 * cols), BF),
            pltpu.VMEM((len(operands), rows, cols), F32),
            pltpu.SemaphoreType.DMA((len(operands),)),
        ],
        compiler_params=pltpu.CompilerParams(vmem_limit_bytes=30 * 2**20),
        cost_estimate=cost(48 * rows * cols * cols, 24 * rows * cols),
        name="gram_far",
    )(near, lhs, *operands)


def total_kernel(parts_ref, out_ref):
    total = parts_ref[0]
    for n in range(1, parts_ref.shape[0]):
        total += parts_ref[n]

    @pl.loop(0, out_ref.shape[0], unroll=4)
    def _(n):
        out_ref[n] = total


def strip_total(parts, copies):
    return pl.pallas_call(
        total_kernel,
        out_shape=jax.ShapeDtypeStruct((copies,) + parts.shape[1:], F32),
        in_specs=[VMEM_SPEC],
        out_specs=VMEM_SPEC,
        compiler_params=pltpu.CompilerParams(vmem_limit_bytes=8 * 2**20),
        cost_estimate=cost(parts.size, 8 * parts.size),
        name="total",
    )(parts)


KEEP = {0: 1, 3: 2, 4: 1, 8: 1}
BASE = {2: 1, 6: 1, 10: 1, 11: 2}
PIECES = ((0, 0), (1, 0), (0, 1), (1, 1), (0, 3), (1, 3), (0, 2), (1, 2))


def finish_kernel(total_rows, y_ref, ga_ref, gb_ref, *rest):
    sources = rest[: 2 * len(PIECES)]
    out_ref, gram, gram_low, state, factor, ordered, held, arrived, other, other_in = rest[
        2 * len(PIECES) :
    ]
    other_copy = pltpu.make_async_copy(gb_ref, other, other_in)
    other_copy.start()
    copies, held_refs = fetched(sources, held, arrived)
    x_refs = [held_refs[2 * n : 2 * n + 2] for n in range(len(PIECES))]
    grams = (ga_ref, other)
    y = y_ref[0]

    diagonal = lax.broadcasted_iota(jnp.int32, (128, 128), 0) == lax.broadcasted_iota(
        jnp.int32, (128, 128), 1
    )

    def block(k, row, b):
        return grams[k][:, row, :, b * 128 : (b + 1) * 128].reshape(128, 128)

    def put(at_row, at_col, value):
        high, low = split(value)
        rows, cols = slice(at_row * 128, at_row * 128 + 128), slice(at_col * 128, at_col * 128 + 128)
        gram[rows, cols] = high
        gram_low[rows, cols] = low

    trace = jnp.zeros((128, 128), F32)
    for k in range(2):
        if k:
            other_copy.wait()
        for row in range(4):
            here = 4 * k + row
            after, before = (row + 1) % 4, (row + 3) % 4
            side = k if row < 2 else 1 - k
            own = block(k, row, 0)
            trace += jnp.where(diagonal, own, 0.0)
            put(here, here, own)
            put(here, 4 * (1 - k) + row, block(k, row, 1))
            for one, two, b in (
                (here, 4 * k + after, 2),
                (4 * (1 - k) + row, 4 * k + after, 3),
                (4 * side + before, 4 * k + after, 4),
            ):
                value = block(k, row, b)
                put(one, two, value)
                put(two, one, value.T)
    energy = jnp.sum(jnp.sum(trace, axis=0, keepdims=True), axis=1, keepdims=True)
    square = NV / (4 * (energy + 1e-06))
    half_square = 0.5 * square

    mine = pl.ds(pl.multiple_of(y * 128, 128), 128)
    column = lax.broadcasted_iota(jnp.int32, (128, NV), 1) - y * 128
    unit = (column == lax.broadcasted_iota(jnp.int32, (128, NV), 0)).astype(F32)
    state[0] = 1.5 * unit - half_square * (gram[mine, :].astype(F32) + gram_low[mine, :].astype(F32))

    @pl.loop(0, 12)
    def _(step):
        current = state[0]
        for at, slot in KEEP.items():

            @pl.when(step == at)
            def _():
                state[slot] = current

        slot = jnp.int32(0)
        for at, value in BASE.items():
            slot = jnp.where(step == at, value, slot)
        high, low = split(current * half_square)
        twice = mm(jnp.concatenate([high, low], axis=0), gram[...])
        product = (twice[:128] + twice[128:]) + mm(high, gram_low[...])
        state[0] = 1.5 * state[slot] - product

    scale = jnp.sqrt(square) * math.sqrt(total_rows)
    high, low = split(state[0].T * scale)
    factor[:, :128] = high
    factor[:, 128:] = low

    def core(k, dy):
        return jnp.where(y < 2, k, 1 - k) if dy == 3 else k

    rhs = jnp.concatenate(
        [
            factor[pl.ds(pl.multiple_of((4 * core(k, dy) + lax.rem(y + dy, 4)) * 128, 128), 128), :]
            for k, dy in PIECES
        ],
        axis=0,
    )
    ordered[...] = rhs
    for copy in copies:
        copy.wait()
    chunk = 512
    half = out_ref.shape[0] // 2
    for part in range(2):

        @pl.loop(0, half // chunk)
        def _(step):
            within = pl.ds(pl.multiple_of(step * chunk, chunk), chunk)
            rows = pl.ds(pl.multiple_of(part * half + step * chunk, chunk), chunk)
            parts = [natural(refs, within, part) for refs in x_refs]
            high, low = split(jnp.concatenate(parts, axis=1))
            full = mm(high, ordered[...])
            cols = full.shape[1] // 2
            out_ref[rows, :] = (full[:, :cols] + full[:, cols:]) + mm(low, ordered[:, :cols])


def finish(total_rows, y, gram_a, gram_b, pieces):
    operands = [chunk for piece in pieces for chunk in piece]
    rows, cols = 2 * operands[0].shape[0], operands[0].shape[1]
    return pl.pallas_call(
        functools.partial(finish_kernel, total_rows),
        out_shape=jax.ShapeDtypeStruct((rows, cols), F32),
        in_specs=[SMEM_SPEC, VMEM_SPEC]
        + [pl.BlockSpec(memory_space=pl.ANY)] * (1 + len(operands)),
        out_specs=VMEM_SPEC,
        scratch_shapes=[
            pltpu.VMEM((NV, NV), BF),
            pltpu.VMEM((NV, NV), BF),
            pltpu.VMEM((3, cols, NV), F32),
            pltpu.VMEM((NV, 2 * cols), BF),
            pltpu.VMEM((NV, 2 * cols), BF),
            pltpu.VMEM((len(operands), rows // 2, cols), F32),
            pltpu.SemaphoreType.DMA((len(operands),)),
            pltpu.VMEM(gram_b.shape, F32),
            pltpu.SemaphoreType.DMA(()),
        ],
        compiler_params=pltpu.CompilerParams(vmem_limit_bytes=40 * 2**20),
        cost_estimate=cost(12 * 6 * cols * NV * NV, 4 * rows * cols * 9),
        name="finish",
    )(y, gram_a, gram_b, *operands)


def on_device(vectors, hamiltonian, column_blocks, live_counts, lower_bound, upper_bound):
    rows_dev, panel_cols = vectors.shape
    block_rows, slot_count, block_size, _ = hamiltonian.shape
    row_count, vec_count = lax.axis_size("row"), lax.axis_size("vec")
    first_row = lax.axis_index("row") * block_rows
    local = (column_blocks - first_row + block_rows) % (block_rows * row_count)
    live = jnp.arange(slot_count, dtype=jnp.int32)[None, :] < live_counts[:, None]
    cols = jnp.where(live, jnp.minimum(local, 3 * block_rows - 1), 3 * block_rows).reshape(-1)
    centre = (upper_bound[0] + lower_bound[0]) / 2
    radius = (upper_bound[0] - lower_bound[0]) / 2
    coef = jnp.stack([centre, 1.0 / radius])
    y = (lax.axis_index("vec") // 2)[None].astype(jnp.int32)

    def from_row(value, step):
        return lax.ppermute(value, "row", [((i + step) % row_count, i) for i in range(row_count)])

    def from_y(value, step):
        return lax.ppermute(
            value, "vec", [((i + 2 * step) % vec_count, i) for i in range(vec_count)]
        )

    def from_last(value):
        return lax.ppermute(
            value, "vec", [((i - 2) % vec_count ^ (i >= 4), i) for i in range(vec_count)]
        )

    def swap(value):
        return lax.ppermute(value, "vec", [(i, i ^ 1) for i in range(vec_count)])

    def across_last(value):
        sources = [(i - 2) % vec_count for i in range(vec_count)]
        return lax.ppermute(value, "vec", [(s ^ (s >= 4), i) for i, s in enumerate(sources)])

    blocks = pack(vectors.reshape(block_rows, block_size, panel_cols))
    split_h = split_blocks(hamiltonian)

    def applied(second, operand, prev=None):
        right = from_row(operand, 1)
        left = from_row(operand, -1)
        return apply_field(second, cols, coef, split_h, left, operand, right, prev)

    own, beside, own_s, up, up_s, down, down_s, across, across_s = ([] for _ in range(9))
    for chunk in range(CHUNKS):
        first = applied(False, blocks[chunk])
        second = applied(True, first, blocks[chunk])
        own.append(second.reshape(rows_dev // 2, panel_cols))
        up.append(from_y(own[-1], 1))
        down.append(from_last(own[-1]))
        beside.append(swap(own[-1]))
        own_s.append(swap(lax.optimization_barrier(own[-1])))
        up_s.append(swap(up[-1]))
        down_s.append(swap(down[-1]))
        across.append(across_last(down[-1]) if chunk else from_y(up[-1], 1))
        across_s.append(swap(across[-1]))
    near, lhs = gram_near((own, beside))
    share = gram_far(near, lhs, (up, down))
    strip = share.shape[0] // row_count
    parts = lax.all_to_all(
        share.reshape(row_count, strip, -1), "row", split_axis=0, concat_axis=0, tiled=True
    )
    groups = [
        [r * vec_count + v for r in range(row_count) for v in range(core, vec_count, 2)]
        for core in range(2)
    ]
    members = row_count * vec_count // 2
    part = strip_total(parts, members)
    gram_a = lax.all_to_all(
        part,
        ("row", "vec"),
        split_axis=0,
        concat_axis=0,
        tiled=True,
        axis_index_groups=groups,
    ).reshape(row_count, vec_count // 2, strip, -1)
    gram_b = swap(gram_a)
    pieces = (own, own_s, up, up_s, down, down_s, across, across_s)
    return finish(rows_dev * row_count, y, gram_a, gram_b, pieces)


def solution(mesh):
    placed = (P("row", "vec"), P("row", None, None, None), P("row", None), P("row"), P(), P())

    return jax.shard_map(
        on_device, mesh=mesh, in_specs=placed, out_specs=P("row", "vec"), check_vma=False
    )
```
